512 devices in a mesh: sa: 32 (over z, core), sb: 16 (over x, y).
Axes of the slice: x: 4, y: 4, z: 16, core: 2. Of those that a mesh axis runs over, the one named last changes fastest.
Arguments:
- queries: bfloat16 [65536, 16, 192], P(('sa', 'sb')), may hold values from -110 to 110
- keys: bfloat16 [65536, 192], P(('sa', 'sb')), may hold values from -6 to 6
- values: bfloat16 [65536, 128], P(('sa', 'sb')), may hold values from -6 to 6
- key_first: bfloat16 [6144, 192], replicated, may hold values from -0.078125 to 0.078125
- key_second: bfloat16 [192, 192], replicated, may hold values from -0.4375 to 0.4375
- value_first: bfloat16 [4096, 128], replicated, may hold values from -0.09375 to 0.09375
- value_second: bfloat16 [128, 128], replicated, may hold values from -0.5 to 0.5
- gate_table: float32 [16, 2], replicated, may hold values from 0.1 to 1
- gate_index: int32 [65536, 16], P(('sa', 'sb')), may hold values from 0 to 15
Outputs:
- mixed: bfloat16 [65536, 16, 128], P(('sa', 'sb'))
The draws below stay inside these ranges and needn't reach their ends.
All inputs are finite; a program needn't handle non-finite values.
Results may differ from the reference program's by a relative error of at most 0.0053.
Values may be sent and summed in bfloat16 or wider, within the bound.
No kernel may reach another device: no remote copies, remote signals or barrier semaphores. Data moves between devices by JAX's collectives and lax.ppermute only.
A program may use at most 64 MiB of HBM per device.

```python
import jax
import jax.numpy as jnp
from jax import lax

HEADS = 16
DK = 192
DV = 128
BLOCK = 32
STRIDE = 16
WINDOW = 512
LEVELS = 16
TOKENS = 65536
NB = 4096


def draw_queries(key, part):
    first = jax.random.fold_in(jax.random.fold_in(key, 11), 0)
    base = 4.0 * jax.random.truncated_normal(first, -6.0, 6.0, (TOKENS, HEADS, DK), jnp.float32)
    return base.astype(jnp.bfloat16)


def touch_ends(array, stream_key, smallest, high):
    spot = [jax.random.randint(jax.random.fold_in(stream_key, axis), (), 0, length) for axis, length in enumerate(array.shape)]
    longest = array.shape.index(max(array.shape))
    neighbour = spot[:longest] + [(spot[longest] + 1) % array.shape[longest]] + spot[longest + 1:]
    return array.at[tuple(spot)].set(smallest).at[tuple(neighbour)].set(high)


def block_levels(stream_key, shape, cuts, smallest, top_value):
    factor_of, own = 1.0, jax.random.fold_in(stream_key, 6)
    for position, parts in cuts:
        heights = jnp.exp(jax.random.uniform(jax.random.fold_in(own, position), (parts,), jnp.float32, smallest / len(cuts), top_value / len(cuts)))
        factor_of = factor_of * jnp.repeat(heights, shape[position] // parts).reshape([-1 if axis == position else 1 for axis in range(len(shape))])
    return factor_of


def gaussian(stream_key, shape, scale, most, cuts=(), kind=jnp.bfloat16):
    values = jax.random.normal(stream_key, shape, jnp.float32) * scale
    if len(cuts) > 0:
        values = block_levels(stream_key, shape, cuts, -0.22, 0.18) * values
    return jnp.clip(values, min=-most, max=most).astype(kind)


def setup_inputs(seed: int = 0) -> dict:
    key_of = jax.random.split(jax.random.key(seed), 10)
    return {
        "queries": draw_queries(jax.random.fold_in(key_of[9], 71), 0),
        "keys": gaussian(key_of[1], (TOKENS, DK), 1.0, 6.0, ((0, 512),)),
        "values": gaussian(key_of[2], (TOKENS, DV), 1.0, 6.0, ((0, 512),)),
        "key_first": gaussian(key_of[3], (BLOCK * DK, DK), (BLOCK * DK) ** -0.5, 0.078125),
        "key_second": gaussian(key_of[4], (DK, DK), DK ** -0.5, 0.4375),
        "value_first": gaussian(key_of[5], (BLOCK * DV, DV), (BLOCK * DV) ** -0.5, 0.09375),
        "value_second": gaussian(key_of[6], (DV, DV), DV ** -0.5, 0.5),
        "gate_table": jnp.clip(jax.random.uniform(key_of[7], (LEVELS, 2), jnp.float32, 0.1, 1.0), 0.1, 1.0),
        "gate_index": touch_ends(jax.random.randint(key_of[8], (TOKENS, HEADS), 0, LEVELS), jax.random.fold_in(key_of[8], 1), 0, LEVELS - 1).astype(jnp.int32),
    }


def compress(rows, first, second):
    width = rows.shape[1]
    padded = jnp.concatenate([jnp.zeros((STRIDE, width), rows.dtype), rows], axis=0)
    front = padded[:TOKENS].reshape(NB, STRIDE * width)
    back = padded[STRIDE:].reshape(NB, STRIDE * width)
    flat = jnp.concatenate([front, back], axis=1)
    hidden = jax.nn.silu(jnp.dot(flat, first, preferred_element_type=jnp.float32)).astype(jnp.bfloat16)
    return jnp.dot(hidden, second, preferred_element_type=jnp.float32).astype(jnp.bfloat16)


def reference(queries, keys, values, key_first, key_second, value_first, value_second, gate_table, gate_index):
    summary_keys = compress(keys, key_first, key_second)
    summary_values = compress(values, value_first, value_second)
    scale = DK ** -0.5
    span = 512
    key_pad = jnp.concatenate([jnp.zeros((WINDOW, DK), keys.dtype), keys], axis=0)
    value_pad = jnp.concatenate([jnp.zeros((WINDOW, DV), values.dtype), values], axis=0)
    block_ends = STRIDE * lax.iota(jnp.int32, NB) + STRIDE - 1

    def one_block(index):
        begin = (index * span).astype(jnp.int32)
        query_rows = lax.dynamic_slice_in_dim(queries, begin, span, 0).reshape(span * HEADS, DK)
        positions = begin + lax.iota(jnp.int32, span * HEADS) // HEADS
        scores = jnp.dot(query_rows, summary_keys.T, preferred_element_type=jnp.float32) * scale
        visible = block_ends[None, :] <= positions[:, None]
        masked = jnp.where(visible, scores, -1e30)
        top = jnp.max(masked, axis=1, keepdims=True)
        weights = jnp.where(visible, jnp.exp(masked - top), 0.0)
        total = jnp.sum(weights, axis=1)
        numer = jnp.dot(weights.astype(jnp.bfloat16), summary_values, preferred_element_type=jnp.float32)
        present = total > 0.0
        compressed = jnp.where(present[:, None], numer / jnp.where(present, total, 1.0)[:, None], 0.0)
        near_keys = lax.dynamic_slice_in_dim(key_pad, begin, span + WINDOW, 0)
        near_values = lax.dynamic_slice_in_dim(value_pad, begin, span + WINDOW, 0)
        key_pos = begin - WINDOW + lax.iota(jnp.int32, span + WINDOW)
        near_scores = jnp.dot(query_rows, near_keys.T, preferred_element_type=jnp.float32) * scale
        inside = (key_pos[None, :] <= positions[:, None]) & (key_pos[None, :] > positions[:, None] - WINDOW) & (key_pos[None, :] >= 0)
        near_masked = jnp.where(inside, near_scores, -1e30)
        near_top = jnp.max(near_masked, axis=1, keepdims=True)
        near_weights = jnp.where(inside, jnp.exp(near_masked - near_top), 0.0)
        near_total = jnp.sum(near_weights, axis=1)
        window = jnp.dot(near_weights.astype(jnp.bfloat16), near_values, preferred_element_type=jnp.float32) / near_total[:, None]
        chosen = lax.dynamic_slice_in_dim(gate_index, begin, span, 0).reshape(span * HEADS)
        onehot = (chosen[:, None] == lax.iota(jnp.int32, LEVELS)[None, :]).astype(jnp.float32)
        gates = jnp.sum(onehot[:, :, None] * gate_table[None, :, :], axis=1)
        mixed = gates[:, 0:1] * compressed + gates[:, 1:2] * window
        return mixed.astype(jnp.bfloat16).reshape(span, HEADS, DV)

    result = lax.map(one_block, jnp.arange(TOKENS // span, dtype=jnp.int32))
    return result.reshape(TOKENS, HEADS, DV)
```

```python
import functools

import jax
import jax.numpy as jnp
from jax import lax
from jax.experimental import pallas as pl
from jax.experimental.pallas import tpu as pltpu
from jax.sharding import PartitionSpec as P

STRIDE = 16
WINDOW = 512
LOG2E = 1.4426950408889634
LOW = -1e30
FLOOR = -1e29


def nt(a, b):
    return lax.dot_general(a, b, (((1,), (1,)), ((), ())), preferred_element_type=jnp.float32)


def shifted(shard, axis, by):
    size = lax.axis_size(axis)
    pairs = [(i, i + by) for i in range(size) if 0 <= i + by < size]
    return lax.ppermute(shard, axis, pairs)


def summarize(padded, first, second, count):
    width = padded.shape[1]
    front = padded[: count * STRIDE].reshape(count, STRIDE * width)
    back = padded[STRIDE:].reshape(count, STRIDE * width)
    flat = jnp.concatenate([front, back], axis=1)
    hidden = jax.nn.silu(jnp.dot(flat, first, preferred_element_type=jnp.float32)).astype(
        jnp.bfloat16
    )
    return jnp.dot(hidden, second, preferred_element_type=jnp.float32).astype(jnp.bfloat16)


def window_kernel(scale, heads, who, q_ref, ctx_ref, gate_ref, out_ref):
    block = q_ref.shape[0]
    rows = block // heads
    local = ctx_ref.shape[0] // 5
    base = pl.program_id(0) * rows
    device = who[0]
    q = q_ref[...]
    q = jnp.concatenate([q, jnp.zeros((block, 64), q.dtype)], axis=1)
    token = base + lax.broadcasted_iota(jnp.int32, (block, local), 0) // heads
    lane = lax.broadcasted_iota(jnp.int32, (block, local), 1)
    scores = []
    for part in range(5):
        s = nt(q, ctx_ref[part * local : (part + 1) * local, 0:256])
        if part == 0:
            s = jnp.where((lane > token) & (device >= 4), s, LOW)
        elif part == 4:
            s = jnp.where(lane <= token, s, LOW)
        else:
            s = jnp.where(device >= 4 - part, s, LOW)
        scores.append(s)
    top = scores[0]
    for s in scores[1:]:
        top = jnp.maximum(top, s)
    top = jnp.maximum(jnp.max(top, axis=1, keepdims=True), FLOOR)
    ones = jnp.ones((local, 128), jnp.bfloat16)
    accum = jnp.zeros((block, 256), jnp.float32)
    for part, s in enumerate(scores):
        p = jnp.exp2((s - top) * (scale * LOG2E)).astype(jnp.bfloat16)
        v = ctx_ref[part * local : (part + 1) * local, 256:384]
        accum += jnp.dot(p, jnp.concatenate([v, ones], axis=1), preferred_element_type=jnp.float32)
    out_ref[...] = gate_ref[:, 1:2] * (accum[:, :128] / accum[:, 128:])


def window_branch(who, q, ctx, gates, scale, heads, block=256):
    total = q.shape[0]
    return pl.pallas_call(
        functools.partial(window_kernel, scale, heads),
        grid_spec=pltpu.PrefetchScalarGridSpec(
            num_scalar_prefetch=1,
            grid=(total // block,),
            in_specs=[
                pl.BlockSpec((block, q.shape[1]), lambda i, w: (i, 0)),
                pl.BlockSpec(ctx.shape, lambda i, w: (0, 0)),
                pl.BlockSpec((block, 2), lambda i, w: (i, 0)),
            ],
            out_specs=pl.BlockSpec((block, 128), lambda i, w: (i, 0)),
        ),
        out_shape=jax.ShapeDtypeStruct((total, 128), jnp.float32),
        name="window",
        cost_estimate=pl.CostEstimate(
            flops=2 * total * 640 * 512, bytes_accessed=3000000, transcendentals=total * 640
        ),
    )(who, q, ctx, gates)


def partial_scores(scale, heads, device, core, q_ref, kv_ref, s_ref, base):
    block = q_ref.shape[0]
    groups = kv_ref.shape[0] // 4
    q = q_ref[...]
    zeros = jnp.zeros((block, 64), q.dtype)
    queries = (
        jnp.concatenate([q, zeros], axis=1),
        jnp.concatenate([q[:, :128], zeros, q[:, 128:]], axis=1),
    )
    token = base + lax.broadcasted_iota(jnp.int32, (block, 256), 0) // heads
    lane = lax.broadcasted_iota(jnp.int32, (1, 256), 1)
    top = None
    for g in range(groups):
        for half in range(2):
            low = kv_ref[4 * g : 4 * g + 4, 64 * half : 64 * half + 64].reshape(256, 128)
            high = kv_ref[4 * g : 4 * g + 4, 128:192].reshape(256, 128)
            s = nt(queries[half], jnp.concatenate([low, high], axis=1))
            z = 8 * half + (lane % 64) // 8
            owner = (2 * z + core) * 16 + 4 * g + lane // 64
            end = (owner - device) * 128 + STRIDE * (lane % 8) + STRIDE - 1
            s = jnp.where(end <= token, s, LOW)
            slot = 2 * g + half
            s_ref[:, 256 * slot : 256 * slot + 256] = s
            most = jnp.maximum(s[:, :128], s[:, 128:])
            top = most if top is None else jnp.maximum(top, most)
    top = jnp.maximum(jnp.max(top, axis=1, keepdims=True), FLOOR)
    ones = jnp.ones((256, 128), jnp.bfloat16)
    accum = jnp.zeros((block, 256), jnp.float32)
    for g in range(groups):
        for half in range(2):
            slot = 2 * g + half
            s = s_ref[:, 256 * slot : 256 * slot + 256]
            p = jnp.exp2((s - top) * (scale * LOG2E)).astype(jnp.bfloat16)
            v = kv_ref[4 * g : 4 * g + 4, 192 + 64 * half : 256 + 64 * half].reshape(256, 128)
            accum += jnp.dot(
                p, jnp.concatenate([v, ones], axis=1), preferred_element_type=jnp.float32
            )
    return accum, top


def first_kernel(scale, heads, who, q_ref, kv_ref, acc_ref, top_ref, s_ref):
    base = pl.program_id(0) * (q_ref.shape[0] // heads)
    accum, top = partial_scores(scale, heads, who[0], who[1], q_ref, kv_ref, s_ref, base)
    acc_ref[...] = accum
    top_ref[...] = jnp.broadcast_to(top, top_ref.shape)


def second_kernel(
    scale, heads, who, q_ref, kv_ref, acc_ref, top_ref, win_ref, gate_ref, out_ref, s_ref
):
    base = pl.program_id(0) * (q_ref.shape[0] // heads)
    accum, top = partial_scores(scale, heads, who[0], 1 - who[1], q_ref, kv_ref, s_ref, base)
    other = top_ref[...]
    most = jnp.maximum(other, top)
    grow = jnp.exp2((other - most) * (scale * LOG2E))
    shrink = jnp.exp2((top - most) * (scale * LOG2E))
    number = acc_ref[:, :128] * grow + accum[:, :128] * shrink
    total = acc_ref[:, 128:] * grow + accum[:, 128:] * shrink
    present = total > 0.0
    compressed = jnp.where(present, number / jnp.where(present, total, 1.0), 0.0)
    out_ref[...] = (gate_ref[:, 0:1] * compressed + win_ref[...]).astype(out_ref.dtype)


def first_half(who, q, kv, scale, heads, block=256):
    total = q.shape[0]
    keys = kv.shape[0] * 128
    return pl.pallas_call(
        functools.partial(first_kernel, scale, heads),
        grid_spec=pltpu.PrefetchScalarGridSpec(
            num_scalar_prefetch=1,
            grid=(total // block,),
            in_specs=[
                pl.BlockSpec((block, q.shape[1]), lambda i, w: (i, 0)),
                pl.BlockSpec(kv.shape, lambda i, w: (0, 0, 0)),
            ],
            out_specs=[
                pl.BlockSpec((block, 256), lambda i, w: (i, 0)),
                pl.BlockSpec((block, 128), lambda i, w: (i, 0)),
            ],
            scratch_shapes=[pltpu.VMEM((block, keys), jnp.float32)],
        ),
        out_shape=[
            jax.ShapeDtypeStruct((total, 256), jnp.float32),
            jax.ShapeDtypeStruct((total, 128), jnp.float32),
        ],
        name="first_half",
        cost_estimate=pl.CostEstimate(
            flops=2 * total * keys * 512, bytes_accessed=3000000, transcendentals=total * keys
        ),
    )(who, q, kv)


def second_half(who, q, kv, acc, top, win, gates, scale, heads, block=256):
    total = q.shape[0]
    keys = kv.shape[0] * 128

    def row(width):
        return pl.BlockSpec((block, width), lambda i, w: (i, 0))

    return pl.pallas_call(
        functools.partial(second_kernel, scale, heads),
        grid_spec=pltpu.PrefetchScalarGridSpec(
            num_scalar_prefetch=1,
            grid=(total // block,),
            in_specs=[
                row(q.shape[1]),
                pl.BlockSpec(kv.shape, lambda i, w: (0, 0, 0)),
                row(256),
                row(128),
                row(128),
                row(2),
            ],
            out_specs=row(128),
            scratch_shapes=[pltpu.VMEM((block, keys), jnp.float32)],
        ),
        out_shape=jax.ShapeDtypeStruct((total, 128), jnp.bfloat16),
        name="second_half",
        cost_estimate=pl.CostEstimate(
            flops=2 * total * keys * 512, bytes_accessed=5000000, transcendentals=total * keys
        ),
    )(who, q, kv, acc, top, win, gates)


def spread(shard, axis, groups=None):
    size = lax.axis_size(axis) if groups is None else len(groups[0])
    copies = jnp.broadcast_to(shard[None], (size,) + shard.shape)
    return lax.all_to_all(copies, axis, 0, 0, axis_index_groups=groups)


def local(
    queries, keys, values, key_first, key_second, value_first, value_second, gate_table, gate_index
):
    rows, heads, depth = queries.shape
    outer, inner = lax.axis_index("sa"), lax.axis_index("sb")
    core = outer % 2
    device = outer * lax.axis_size("sb") + inner
    who = jnp.stack([device, core]).astype(jnp.int32)
    planes = lax.axis_size("sa") // 2
    scale = depth ** (-0.5)
    gap = jnp.zeros((rows, 64), keys.dtype)
    paired = jnp.concatenate([keys, gap, values], axis=1)
    one = shifted(paired, ("sa", "sb"), 1)
    padded = jnp.concatenate([one[rows - STRIDE :], paired], axis=0)
    count = rows // STRIDE
    key_summary = summarize(padded[:, :depth], key_first, key_second, count)
    value_summary = summarize(padded[:, 256:], value_first, value_second, count)
    payload = jnp.concatenate(
        [
            key_summary[:, :128],
            jnp.pad(key_summary[:, 128:], ((0, 0), (0, 64))),
            value_summary,
        ],
        axis=0,
    )
    column = spread(payload, "sa", [[2 * z + c for z in range(planes)] for c in range(2)])
    high = column[:, 8:16, :64]
    packed = jnp.concatenate(
        [
            column[:, :8].reshape(128, 128),
            jnp.concatenate([high[:8].reshape(64, 64), high[8:].reshape(64, 64)], axis=1),
            column[:, 16:].reshape(128, 128),
        ],
        axis=0,
    )
    mine = spread(packed, "sb")
    other = lax.ppermute(mine, "sa", [(i, i ^ 1) for i in range(2 * planes)])

    two = shifted(jnp.concatenate([one, paired], axis=0), ("sa", "sb"), 2)
    four = shifted(paired, ("sa", "sb"), 4)
    context = jnp.concatenate([four, two, one, paired], axis=0)
    query_rows = queries.reshape(rows * heads, depth)
    chosen = gate_index.reshape(rows * heads)
    onehot = (chosen[:, None] == lax.iota(jnp.int32, gate_table.shape[0])[None, :]).astype(
        jnp.float32
    )
    gates = jnp.sum(onehot[:, :, None] * gate_table[None, :, :], axis=1)
    win = window_branch(who, query_rows, context, gates, scale, heads)
    acc, top = first_half(who, query_rows, mine, scale, heads)
    mixed = second_half(who, query_rows, other, acc, top, win, gates, scale, heads)
    return mixed.reshape(rows, heads, values.shape[1])


def solution(mesh):
    in_specs = (
        P(("sa", "sb"), None, None),
        P(("sa", "sb"), None),
        P(("sa", "sb"), None),
        P(),
        P(),
        P(),
        P(),
        P(),
        P(("sa", "sb"), None),
    )
    out_specs = P(("sa", "sb"), None, None)
    return jax.shard_map(local, mesh=mesh, in_specs=in_specs, out_specs=out_specs, check_vma=False)
```

```python
import functools

import jax
import jax.numpy as jnp
from jax import lax
from jax.experimental import pallas as pl
from jax.experimental.pallas import tpu as pltpu
from jax.sharding import PartitionSpec as P

STRIDE = 16
WINDOW = 512
LOG2E = 1.4426950408889634
LOW = -1e30
FLOOR = -1e29
GRANT = 20 << 20


def nt(a, b):
    return lax.dot_general(a, b, (((1,), (1,)), ((), ())), preferred_element_type=jnp.float32)


def shifted(shard, axis, by):
    size = lax.axis_size(axis)
    pairs = [(i, i + by) for i in range(size) if 0 <= i + by < size]
    return lax.ppermute(shard, axis, pairs)


def pair_kernel(keys_ref, values_ref, out_ref):
    out_ref[:, :192] = keys_ref[...].astype(jnp.float32).T.astype(out_ref.dtype)
    out_ref[:, 192:256] = jnp.zeros((out_ref.shape[0], 64), out_ref.dtype)
    out_ref[:, 256:] = values_ref[...]


def pair(keys, values):
    return pl.pallas_call(
        pair_kernel,
        in_specs=[pl.BlockSpec(memory_space=pltpu.VMEM)] * 2,
        out_specs=pl.BlockSpec(memory_space=pltpu.VMEM),
        out_shape=jax.ShapeDtypeStruct((keys.shape[0], 384), keys.dtype),
        compiler_params=pltpu.CompilerParams(vmem_limit_bytes=GRANT),
        name="pair",
    )(keys.T, values)


def silu(x):
    return x * (1.0 / (1.0 + jnp.exp(-x)))


def segments(wide_ref, count):
    keys, values = [], []
    for first in range(STRIDE):
        some = [wide_ref[part, pl.ds(first, count, stride=STRIDE), :] for part in range(3)]
        keys.append(jnp.concatenate([some[0], some[1][:, :64]], axis=1))
        values.append(some[2])
    keys = jnp.concatenate(keys, axis=1).astype(jnp.bfloat16)
    values = jnp.concatenate(values, axis=1).astype(jnp.bfloat16)
    return keys, values


def own_kernel(pair_ref, kfirst_ref, vfirst_ref, hidden_ref, wide):
    half_keys = kfirst_ref.shape[1] // 2
    half_values = vfirst_ref.shape[0] // 2
    count = pair_ref.shape[0] // STRIDE
    for part in range(3):
        lanes = slice(128 * part, 128 * part + 128)
        wide[part] = pair_ref[:, lanes].astype(jnp.float32)
    keys, values = segments(wide, count)
    nothing = jnp.zeros((count, 64), jnp.float32)
    back = jnp.concatenate(
        [
            nt(keys, kfirst_ref[:, half_keys:]),
            nothing,
            jnp.dot(values, vfirst_ref[half_values:], preferred_element_type=jnp.float32),
        ],
        axis=1,
    )
    ahead = jnp.concatenate(
        [
            nt(keys, kfirst_ref[:, :half_keys]),
            nothing,
            jnp.dot(values, vfirst_ref[:half_values], preferred_element_type=jnp.float32),
        ],
        axis=1,
    )
    row = lax.broadcasted_iota(jnp.int32, back.shape, 0)
    hidden_ref[...] = back + jnp.where(row == 0, 0.0, pltpu.roll(ahead, 1, 0))


def own_blocks(paired, kfirst, vfirst):
    rows = paired.shape[0]
    inside = pl.BlockSpec(memory_space=pltpu.VMEM)
    return pl.pallas_call(
        own_kernel,
        in_specs=[inside] * 3,
        out_specs=inside,
        out_shape=jax.ShapeDtypeStruct((rows // STRIDE, 384), jnp.float32),
        scratch_shapes=[pltpu.VMEM((3, rows, 128), jnp.float32)],
        compiler_params=pltpu.CompilerParams(vmem_limit_bytes=GRANT),
        name="own_blocks",
        cost_estimate=pl.CostEstimate(
            flops=1000000000, bytes_accessed=8000000, transcendentals=0
        ),
    )(paired, kfirst, vfirst)


def summary_kernel(
    before_ref, hidden_ref, kfirst_ref, ksecond_ref, vfirst_ref, vsecond_ref, out_ref, wide
):
    rows = before_ref.shape[0]
    count = hidden_ref.shape[0]
    for part in range(3):
        lanes = slice(128 * part, 128 * part + 128)
        wide[part] = before_ref[:, lanes].astype(jnp.float32)
    keys, values = segments(wide, rows // STRIDE)
    ahead = jnp.concatenate(
        [
            nt(keys, kfirst_ref[:, : kfirst_ref.shape[1] // 2]),
            jnp.zeros((count, 64), jnp.float32),
            jnp.dot(
                values,
                vfirst_ref[: vfirst_ref.shape[0] // 2],
                preferred_element_type=jnp.float32,
            ),
        ],
        axis=1,
    )
    row = lax.broadcasted_iota(jnp.int32, ahead.shape, 0)
    hidden = hidden_ref[...] + jnp.where(row == 0, pltpu.roll(ahead, 1, 0), 0.0)
    hidden = silu(hidden).astype(jnp.bfloat16)
    key = jnp.dot(hidden[:, :192], ksecond_ref[...], preferred_element_type=jnp.float32)
    value = jnp.dot(hidden[:, 256:], vsecond_ref[...], preferred_element_type=jnp.float32)
    high = jnp.concatenate([key[:, 128:], jnp.zeros((count, 64), jnp.float32)], axis=1)
    payload = jnp.concatenate([key[:, :128], high, value], axis=0).astype(out_ref.dtype)
    for copy in range(out_ref.shape[0]):
        out_ref[copy] = payload


def summary(before, hidden, kfirst, key_second, vfirst, value_second, copies):
    inside = pl.BlockSpec(memory_space=pltpu.VMEM)
    default = pl.BlockSpec()
    return pl.pallas_call(
        summary_kernel,
        in_specs=[inside, inside, inside, default, inside, default],
        out_specs=inside,
        out_shape=jax.ShapeDtypeStruct((copies, 3 * hidden.shape[0], 128), jnp.bfloat16),
        scratch_shapes=[pltpu.VMEM((3,) + (before.shape[0], 128), jnp.float32)],
        compiler_params=pltpu.CompilerParams(vmem_limit_bytes=GRANT),
        name="summary",
    )(before, hidden, kfirst, key_second, vfirst, value_second)


def window_kernel(
    scale, heads, who, q_ref, four_ref, two_ref, one_ref, pair_ref, gate_ref, out_ref, *scratch
):
    sub = scratch[0].shape[0]
    size = pair_ref.shape[0]
    blocks = q_ref.shape[0] // sub
    device = who[0]
    base = pl.program_id(0) * (q_ref.shape[0] // heads)
    near = (
        jnp.concatenate([four_ref[...], two_ref[:size]], axis=0),
        jnp.concatenate([two_ref[size:], one_ref[...]], axis=0),
        pair_ref[...],
    )
    begins = [
        size * jnp.clip(4 - device, 0, 2),
        size * jnp.clip(2 - device, 0, 2),
    ]

    def score(j):
        s_ref = scratch[j % 2]
        q = q_ref[j * sub : (j + 1) * sub]
        q = jnp.concatenate([q, jnp.zeros((sub, 64), q.dtype)], axis=1)
        token = base + j * (sub // heads) + lax.broadcasted_iota(jnp.int32, (sub, 256), 0) // heads
        lane = lax.broadcasted_iota(jnp.int32, (sub, 256), 1)
        s0 = nt(q, near[0][:, :256])
        s0 = jnp.where(lane > jnp.maximum(token, begins[0] - 1), s0, LOW)
        s1 = nt(q, near[1][:, :256])
        s1 = jnp.where(lane >= begins[1], s1, LOW)
        s2 = nt(q, near[2][:, :256])
        s2 = jnp.where(lane[:, :128] <= token[:, :128], s2, LOW)
        s_ref[:, :256] = s0
        s_ref[:, 256:512] = s1
        s_ref[:, 512:] = s2
        top = jnp.maximum(jnp.maximum(s0, s1), jnp.concatenate([s2, s2], axis=1))
        return jnp.maximum(jnp.max(top, axis=1, keepdims=True), FLOOR)

    def mix(j, top):
        s_ref = scratch[j % 2]
        accum = jnp.zeros((sub, 256), jnp.float32)
        for part, at in enumerate((0, 256, 512)):
            wide = near[part].shape[0]
            p = jnp.exp2((s_ref[:, at : at + wide] - top) * (scale * LOG2E)).astype(jnp.bfloat16)
            v = jnp.concatenate([near[part][:, 256:], jnp.ones((wide, 128), jnp.bfloat16)], axis=1)
            accum += jnp.dot(p, v, preferred_element_type=jnp.float32)
        here = slice(j * sub, (j + 1) * sub)
        out_ref[here] = gate_ref[here, 1:2] * (accum[:, :128] / accum[:, 128:])

    tops = [score(0)]
    for j in range(blocks):
        if j + 1 < blocks:
            tops.append(score(j + 1))
        mix(j, tops[j])


def window_branch(who, q, four, two, one, paired, gates, scale, heads, block=1024, sub=256):
    total = q.shape[0]

    def row(width):
        return pl.BlockSpec((block, width), lambda i, w: (i, 0))

    def whole(array):
        return pl.BlockSpec(array.shape, lambda i, w: (0, 0))

    return pl.pallas_call(
        functools.partial(window_kernel, scale, heads),
        grid_spec=pltpu.PrefetchScalarGridSpec(
            num_scalar_prefetch=1,
            grid=(total // block,),
            in_specs=[
                row(q.shape[1]),
                whole(four),
                whole(two),
                whole(one),
                whole(paired),
                row(2),
            ],
            out_specs=row(128),
            scratch_shapes=[pltpu.VMEM((sub, 640), jnp.float32)] * 2,
        ),
        out_shape=jax.ShapeDtypeStruct((total, 128), jnp.float32),
        compiler_params=pltpu.CompilerParams(vmem_limit_bytes=GRANT),
        name="window",
        cost_estimate=pl.CostEstimate(
            flops=2 * total * 640 * 512, bytes_accessed=4000000, transcendentals=total * 640
        ),
    )(who, q, four, two, one, paired, gates)


def far_scores(heads, device, core, q, kv_ref, s_ref, base):
    block = q.shape[0]
    zeros = jnp.zeros((block, 64), q.dtype)
    queries = (
        jnp.concatenate([q, zeros], axis=1),
        jnp.concatenate([q[:, :128], zeros, q[:, 128:]], axis=1),
    )
    token = base + lax.broadcasted_iota(jnp.int32, (block, 256), 0) // heads
    lane = lax.broadcasted_iota(jnp.int32, (1, 256), 1)
    top = None
    for g in range(kv_ref.shape[0] // 4):
        for half in range(2):
            low = kv_ref[4 * g : 4 * g + 4, 64 * half : 64 * half + 64].reshape(256, 128)
            high = kv_ref[4 * g : 4 * g + 4, 128:192].reshape(256, 128)
            s = nt(queries[half], jnp.concatenate([low, high], axis=1))
            z = 8 * half + (lane % 64) // 8
            owner = (2 * z + core) * 16 + 4 * g + lane // 64
            end = (owner - device) * 128 + STRIDE * (lane % 8) + STRIDE - 1
            s = jnp.where(end <= token, s, LOW)
            slot = 2 * g + half
            s_ref[:, 256 * slot : 256 * slot + 256] = s
            most = jnp.maximum(s[:, :128], s[:, 128:])
            top = most if top is None else jnp.maximum(top, most)
    return jnp.maximum(jnp.max(top, axis=1, keepdims=True), FLOOR)


def far_mix(scale, s_ref, top, kv_ref):
    ones = jnp.ones((256, 128), jnp.bfloat16)
    accum = jnp.zeros((s_ref.shape[0], 256), jnp.float32)
    for g in range(kv_ref.shape[0] // 4):
        for half in range(2):
            slot = 2 * g + half
            s = s_ref[:, 256 * slot : 256 * slot + 256]
            p = jnp.exp2((s - top) * (scale * LOG2E)).astype(jnp.bfloat16)
            v = kv_ref[4 * g : 4 * g + 4, 192 + 64 * half : 256 + 64 * half].reshape(256, 128)
            accum += jnp.dot(
                p, jnp.concatenate([v, ones], axis=1), preferred_element_type=jnp.float32
            )
    return accum


def skewed(scale, heads, device, core, q_ref, kv_ref, scratch, finish):
    sub = scratch[0].shape[0]
    blocks = q_ref.shape[0] // sub
    base = pl.program_id(0) * (q_ref.shape[0] // heads)

    def score(j):
        return far_scores(
            heads,
            device,
            core,
            q_ref[j * sub : (j + 1) * sub],
            kv_ref,
            scratch[j % 2],
            base + j * (sub // heads),
        )

    tops = [score(0)]
    for j in range(blocks):
        if j + 1 < blocks:
            tops.append(score(j + 1))
        finish(slice(j * sub, (j + 1) * sub), far_mix(scale, scratch[j % 2], tops[j], kv_ref), tops[j])


def first_kernel(scale, heads, who, q_ref, kv_ref, acc_ref, top_ref, *scratch):
    def finish(here, accum, top):
        acc_ref[here] = accum
        top_ref[here] = jnp.broadcast_to(top, (accum.shape[0], 128))

    skewed(scale, heads, who[0], who[1], q_ref, kv_ref, scratch, finish)


def second_kernel(
    scale, heads, who, q_ref, kv_ref, acc_ref, top_ref, win_ref, gate_ref, out_ref, *scratch
):
    def finish(here, accum, top):
        other = top_ref[here]
        most = jnp.maximum(other, top)
        grow = jnp.exp2((other - most) * (scale * LOG2E))
        shrink = jnp.exp2((top - most) * (scale * LOG2E))
        number = acc_ref[here, :128] * grow + accum[:, :128] * shrink
        total = acc_ref[here, 128:] * grow + accum[:, 128:] * shrink
        present = total > 0.0
        compressed = jnp.where(present, number / jnp.where(present, total, 1.0), 0.0)
        out_ref[here] = (gate_ref[here, 0:1] * compressed + win_ref[here]).astype(out_ref.dtype)

    skewed(scale, heads, who[0], 1 - who[1], q_ref, kv_ref, scratch, finish)


def first_half(who, q, kv, scale, heads, block=1024, sub=256):
    total = q.shape[0]
    keys = kv.shape[0] * 128
    return pl.pallas_call(
        functools.partial(first_kernel, scale, heads),
        grid_spec=pltpu.PrefetchScalarGridSpec(
            num_scalar_prefetch=1,
            grid=(total // block,),
            in_specs=[
                pl.BlockSpec((block, q.shape[1]), lambda i, w: (i, 0)),
                pl.BlockSpec(memory_space=pltpu.VMEM),
            ],
            out_specs=[
                pl.BlockSpec((block, 256), lambda i, w: (i, 0)),
                pl.BlockSpec((block, 128), lambda i, w: (i, 0)),
            ],
            scratch_shapes=[pltpu.VMEM((sub, keys), jnp.float32)] * 2,
        ),
        out_shape=[
            jax.ShapeDtypeStruct((total, 256), jnp.float32),
            jax.ShapeDtypeStruct((total, 128), jnp.float32),
        ],
        compiler_params=pltpu.CompilerParams(vmem_limit_bytes=GRANT),
        name="first_half",
        cost_estimate=pl.CostEstimate(
            flops=2 * total * keys * 512, bytes_accessed=3000000, transcendentals=total * keys
        ),
    )(who, q, kv)


def second_half(who, q, kv, acc, top, win, gates, scale, heads, block=1024, sub=256):
    total = q.shape[0]
    keys = kv.shape[0] * 128

    def row(width):
        return pl.BlockSpec((block, width), lambda i, w: (i, 0))

    return pl.pallas_call(
        functools.partial(second_kernel, scale, heads),
        grid_spec=pltpu.PrefetchScalarGridSpec(
            num_scalar_prefetch=1,
            grid=(total // block,),
            in_specs=[
                row(q.shape[1]),
                pl.BlockSpec(memory_space=pltpu.VMEM),
                row(256),
                row(128),
                row(128),
                row(2),
            ],
            out_specs=row(128),
            scratch_shapes=[pltpu.VMEM((sub, keys), jnp.float32)] * 2,
        ),
        out_shape=jax.ShapeDtypeStruct((total, 128), jnp.bfloat16),
        compiler_params=pltpu.CompilerParams(vmem_limit_bytes=GRANT),
        name="second_half",
        cost_estimate=pl.CostEstimate(
            flops=2 * total * keys * 512, bytes_accessed=5000000, transcendentals=total * keys
        ),
    )(who, q, kv, acc, top, win, gates)


def local(
    queries, keys, values, key_first, key_second, value_first, value_second, gate_table, gate_index
):
    rows, heads, depth = queries.shape
    outer, inner = lax.axis_index("sa"), lax.axis_index("sb")
    core = outer % 2
    device = outer * lax.axis_size("sb") + inner
    who = jnp.stack([device, core]).astype(jnp.int32)
    planes = lax.axis_size("sa") // 2
    scale = depth ** (-0.5)
    paired = pair(keys, values)
    one = shifted(paired, ("sa", "sb"), 1)
    kfirst = key_first.T
    hidden = own_blocks(paired, kfirst, value_first)
    payload = summary(one, hidden, kfirst, key_second, value_first, value_second, planes)
    payload, later = lax.optimization_barrier((payload, one))
    groups = [[2 * z + c for z in range(planes)] for c in range(2)]
    column = lax.all_to_all(payload, "sa", 0, 0, axis_index_groups=groups)

    two = shifted(jnp.concatenate([later, paired], axis=0), ("sa", "sb"), 2)
    four = shifted(paired, ("sa", "sb"), 4)
    query_rows = queries.reshape(rows * heads, depth)
    chosen = gate_index.reshape(rows * heads)
    onehot = (chosen[:, None] == lax.iota(jnp.int32, gate_table.shape[0])[None, :]).astype(
        jnp.float32
    )
    gates = jnp.sum(onehot[:, :, None] * gate_table[None, :, :], axis=1)
    column, two, four, query_rows, gates = lax.optimization_barrier(
        (column, two, four, query_rows, gates)
    )

    high = column[:, 8:16, :64]
    packed = jnp.concatenate(
        [
            column[:, :8].reshape(128, 128),
            jnp.concatenate([high[:8].reshape(64, 64), high[8:].reshape(64, 64)], axis=1),
            column[:, 16:].reshape(128, 128),
        ],
        axis=0,
    )
    copies = jnp.broadcast_to(packed[None], (lax.axis_size("sb"),) + packed.shape)
    mine = lax.all_to_all(copies, "sb", 0, 0)
    win = window_branch(who, query_rows, four, two, later, paired, gates, scale, heads)
    mine, win = lax.optimization_barrier((mine, win))
    other = lax.ppermute(mine, "sa", [(i, i ^ 1) for i in range(2 * planes)])
    acc, top = first_half(who, query_rows, mine, scale, heads)
    mixed = second_half(who, query_rows, other, acc, top, win, gates, scale, heads)
    return mixed.reshape(rows, heads, values.shape[1])


def solution(mesh):
    in_specs = (
        P(("sa", "sb"), None, None),
        P(("sa", "sb"), None),
        P(("sa", "sb"), None),
        P(),
        P(),
        P(),
        P(),
        P(),
        P(("sa", "sb"), None),
    )
    out_specs = P(("sa", "sb"), None, None)
    return jax.shard_map(local, mesh=mesh, in_specs=in_specs, out_specs=out_specs, check_vma=False)
```

```python
import functools

import jax
import jax.numpy as jnp
from jax import lax
from jax.experimental import pallas as pl
from jax.experimental.pallas import tpu as pltpu
from jax.sharding import PartitionSpec as P


STRIDE = 16
LOG2E = 1.4426950408889634
LOW = -1e30
FLOOR = -1e29
GRANT = 20 << 20
PAIR_GRANT = 63400000


def nt(a, b):
    return lax.dot_general(a, b, (((1,), (1,)), ((), ())), preferred_element_type=jnp.float32)


def shifted(shard, axis, by):
    size = lax.axis_size(axis)
    pairs = [(i, i + by) for i in range(size) if 0 <= i + by < size]
    return lax.ppermute(shard, axis, pairs)


def pair_kernel(keys_hbm, values_hbm, out_ref, keys, sems):
    loads = [
        pltpu.make_async_copy(keys_hbm, keys, sems.at[0]),
        pltpu.make_async_copy(values_hbm, out_ref.at[:, 256:], sems.at[1]),
    ]
    for load in loads:
        load.start()
    out_ref[:, 192:256] = jnp.zeros((out_ref.shape[0], 64), out_ref.dtype)
    loads[0].wait()
    out_ref[:, :192] = keys[...].astype(jnp.float32).T.astype(out_ref.dtype)
    loads[1].wait()


def pair(keys, values):
    anywhere = pl.BlockSpec(memory_space=pl.ANY)
    return pl.pallas_call(
        pair_kernel,
        in_specs=[anywhere, anywhere],
        out_specs=pl.BlockSpec(memory_space=pltpu.VMEM),
        out_shape=jax.ShapeDtypeStruct((keys.shape[0], 384), keys.dtype),
        scratch_shapes=[
            pltpu.VMEM((keys.shape[1], keys.shape[0]), keys.dtype),
            pltpu.SemaphoreType.DMA((2,)),
        ],
        compiler_params=pltpu.CompilerParams(vmem_limit_bytes=PAIR_GRANT),
        name="pair",
    )(keys.T, values)


def silu(x):
    return x * (1.0 / (1.0 + jnp.exp(-x)))


def flatten(wide, count):
    keys, values = [], []
    for first in range(STRIDE):
        some = [wide[part, pl.ds(first, count, stride=STRIDE), :] for part in range(3)]
        keys.append(jnp.concatenate([some[0], some[1][:, :64]], axis=1))
        values.append(some[2])
    keys = jnp.concatenate(keys, axis=1).astype(jnp.bfloat16)
    values = jnp.concatenate(values, axis=1).astype(jnp.bfloat16)
    return keys, values


def first_layer(keys, values, waits, kfirst_ref, vfirst_ref):
    piece = kfirst_ref.shape[1] // 2
    total = None
    for part in range(2):
        waits[part].wait()
        lanes = slice(part * piece, part * piece + piece)
        some = nt(keys[:, lanes], kfirst_ref[:, lanes])
        total = some if total is None else total + some
    waits[2].wait()
    value = jnp.dot(values, vfirst_ref[...], preferred_element_type=jnp.float32)
    nothing = jnp.zeros((keys.shape[0], 64), jnp.float32)
    return jnp.concatenate([total, nothing, value], axis=1)


def load_half(half, kfirst_hbm, vfirst_hbm, kfirst_ref, vfirst_ref, sems):
    wide, tall = kfirst_ref.shape[1], vfirst_ref.shape[0]
    piece = wide // 2
    loads = [
        pltpu.make_async_copy(
            kfirst_hbm.at[:, half * wide + part * piece : half * wide + (part + 1) * piece],
            kfirst_ref.at[:, part * piece : (part + 1) * piece],
            sems.at[part],
        )
        for part in range(2)
    ]
    loads.append(
        pltpu.make_async_copy(
            vfirst_hbm.at[half * tall : (half + 1) * tall], vfirst_ref, sems.at[2]
        )
    )
    for load in loads:
        load.start()
    return loads


def own_kernel(
    pair_ref, kfirst_hbm, vfirst_hbm, hidden_ref, wide, kback, vback, kfront, vfront, sems
):
    back_loads = load_half(1, kfirst_hbm, vfirst_hbm, kback, vback, sems.at[0])
    front_loads = load_half(0, kfirst_hbm, vfirst_hbm, kfront, vfront, sems.at[1])
    count = pair_ref.shape[0] // STRIDE
    for part in range(3):
        lanes = slice(128 * part, 128 * part + 128)
        wide[part] = pair_ref[:, lanes].astype(jnp.float32)
    keys, values = flatten(wide, count)
    back = first_layer(keys, values, back_loads, kback, vback)
    ahead = first_layer(keys, values, front_loads, kfront, vfront)
    row = lax.broadcasted_iota(jnp.int32, back.shape, 0)
    hidden_ref[...] = back + jnp.where(row == 0, 0.0, pltpu.roll(ahead, 1, 0))


def own_blocks(paired, kfirst, vfirst):
    rows = paired.shape[0]
    inside = pl.BlockSpec(memory_space=pltpu.VMEM)
    anywhere = pl.BlockSpec(memory_space=pl.ANY)
    khalf = pltpu.VMEM((kfirst.shape[0], kfirst.shape[1] // 2), jnp.bfloat16)
    vhalf = pltpu.VMEM((vfirst.shape[0] // 2, vfirst.shape[1]), jnp.bfloat16)
    return pl.pallas_call(
        own_kernel,
        in_specs=[inside, anywhere, anywhere],
        out_specs=inside,
        out_shape=jax.ShapeDtypeStruct((rows // STRIDE, 384), jnp.float32),
        scratch_shapes=[
            pltpu.VMEM((3, rows, 128), jnp.float32),
            khalf,
            vhalf,
            khalf,
            vhalf,
            pltpu.SemaphoreType.DMA((2, 3)),
        ],
        compiler_params=pltpu.CompilerParams(vmem_limit_bytes=PAIR_GRANT),
        name="own_blocks",
        cost_estimate=pl.CostEstimate(
            flops=1000000000, bytes_accessed=8000000, transcendentals=0
        ),
    )(paired, kfirst, vfirst)


def summary_kernel(
    before_hbm,
    hidden_ref,
    kfirst_hbm,
    ksecond_hbm,
    vfirst_hbm,
    vsecond_hbm,
    out_ref,
    before,
    wide,
    kfront,
    vfront,
    ksecond,
    vsecond,
    sems,
    more,
):
    rows = before_hbm.shape[0]
    count = hidden_ref.shape[0]
    halo = pltpu.make_async_copy(before_hbm.at[rows - STRIDE :], before, more.at[0])
    halo.start()
    front_loads = load_half(0, kfirst_hbm, vfirst_hbm, kfront, vfront, sems)
    seconds = [
        pltpu.make_async_copy(ksecond_hbm, ksecond, more.at[1]),
        pltpu.make_async_copy(vsecond_hbm, vsecond, more.at[2]),
    ]
    for load in seconds:
        load.start()
    halo.wait()
    wide[...] = jnp.zeros_like(wide)
    for part in range(3):
        lanes = slice(128 * part, 128 * part + 128)
        wide[part, :STRIDE] = before[:, lanes].astype(jnp.float32)
    keys, values = flatten(wide, count)
    ahead = first_layer(keys, values, front_loads, kfront, vfront)
    row = lax.broadcasted_iota(jnp.int32, ahead.shape, 0)
    hidden = hidden_ref[...] + jnp.where(row == 0, ahead, 0.0)
    hidden = silu(hidden).astype(jnp.bfloat16)
    for load in seconds:
        load.wait()
    key = jnp.dot(hidden[:, :192], ksecond[...], preferred_element_type=jnp.float32)
    value = jnp.dot(hidden[:, 256:], vsecond[...], preferred_element_type=jnp.float32)
    high = jnp.concatenate([key[:, 128:], jnp.zeros((count, 64), jnp.float32)], axis=1)
    payload = jnp.concatenate([key[:, :128], high, value], axis=0).astype(out_ref.dtype)
    for copy in range(out_ref.shape[0]):
        out_ref[copy] = payload


def summary(before, hidden, kfirst, ksecond, vfirst, vsecond, copies):
    count = hidden.shape[0]
    inside = pl.BlockSpec(memory_space=pltpu.VMEM)
    anywhere = pl.BlockSpec(memory_space=pl.ANY)
    return pl.pallas_call(
        summary_kernel,
        in_specs=[anywhere, inside] + [anywhere] * 4,
        out_specs=inside,
        out_shape=jax.ShapeDtypeStruct((copies, 3 * count, 128), jnp.bfloat16),
        scratch_shapes=[
            pltpu.VMEM((STRIDE, before.shape[1]), jnp.bfloat16),
            pltpu.VMEM((3, before.shape[0], 128), jnp.float32),
            pltpu.VMEM((kfirst.shape[0], kfirst.shape[1] // 2), jnp.bfloat16),
            pltpu.VMEM((vfirst.shape[0] // 2, vfirst.shape[1]), jnp.bfloat16),
            pltpu.VMEM(ksecond.shape, jnp.bfloat16),
            pltpu.VMEM(vsecond.shape, jnp.bfloat16),
            pltpu.SemaphoreType.DMA((3,)),
            pltpu.SemaphoreType.DMA((3,)),
        ],
        compiler_params=pltpu.CompilerParams(vmem_limit_bytes=PAIR_GRANT),
        name="summary",
    )(before, hidden, kfirst, ksecond, vfirst, vsecond)


def pack_kernel(column_ref, out_ref):
    planes = column_ref.shape[0]
    half = planes // 2
    count = column_ref.shape[1] // 3
    low = column_ref[:, :count].astype(jnp.float32).reshape(planes * count, 128)
    high = column_ref[:, count : 2 * count].astype(jnp.float32)
    high = jnp.concatenate(
        [
            high[:half].reshape(half * count, 128)[:, :64],
            high[half:].reshape(half * count, 128)[:, :64],
        ],
        axis=1,
    )
    value = column_ref[:, 2 * count :].astype(jnp.float32).reshape(planes * count, 128)
    packed = jnp.concatenate([low, high, value], axis=0).astype(out_ref.dtype)
    for copy in range(out_ref.shape[0]):
        out_ref[copy] = packed


def pack(column, copies):
    planes, rows, lanes = column.shape
    inside = pl.BlockSpec(memory_space=pltpu.VMEM)
    return pl.pallas_call(
        pack_kernel,
        in_specs=[inside],
        out_specs=inside,
        out_shape=jax.ShapeDtypeStruct((copies, planes * rows * 5 // 6, lanes), column.dtype),
        compiler_params=pltpu.CompilerParams(vmem_limit_bytes=GRANT),
        name="pack",
    )(column)


def window_kernel(
    scale, heads, who, q_ref, four_ref, two_ref, one_ref, pair_ref, gate_ref, out_ref, *scratch
):
    sub = scratch[0].shape[0]
    size = pair_ref.shape[0]
    blocks = q_ref.shape[0] // sub
    device = who[0]
    base = pl.program_id(0) * (q_ref.shape[0] // heads)
    near = (
        jnp.concatenate([four_ref[...], two_ref[:size]], axis=0),
        jnp.concatenate([two_ref[size:], one_ref[...]], axis=0),
        pair_ref[...],
    )
    begins = [
        size * jnp.clip(4 - device, 0, 2),
        size * jnp.clip(2 - device, 0, 2),
    ]

    def score(j):
        s_ref = scratch[j % 2]
        q = q_ref[j * sub : (j + 1) * sub]
        q = jnp.concatenate([q, jnp.zeros((sub, 64), q.dtype)], axis=1)
        token = base + j * (sub // heads) + lax.broadcasted_iota(jnp.int32, (sub, 256), 0) // heads
        lane = lax.broadcasted_iota(jnp.int32, (sub, 256), 1)
        s0 = nt(q, near[0][:, :256])
        s0 = jnp.where(lane > jnp.maximum(token, begins[0] - 1), s0, LOW)
        s1 = nt(q, near[1][:, :256])
        s1 = jnp.where(lane >= begins[1], s1, LOW)
        s2 = nt(q, near[2][:, :256])
        s2 = jnp.where(lane[:, :128] <= token[:, :128], s2, LOW)
        s_ref[:, :256] = s0
        s_ref[:, 256:512] = s1
        s_ref[:, 512:] = s2
        top = jnp.maximum(jnp.maximum(s0, s1), jnp.concatenate([s2, s2], axis=1))
        return jnp.maximum(jnp.max(top, axis=1, keepdims=True), FLOOR)

    def mix(j, top):
        s_ref = scratch[j % 2]
        accum = jnp.zeros((sub, 256), jnp.float32)
        for part, at in enumerate((0, 256, 512)):
            wide = near[part].shape[0]
            p = jnp.exp2((s_ref[:, at : at + wide] - top) * (scale * LOG2E)).astype(jnp.bfloat16)
            v = jnp.concatenate([near[part][:, 256:], jnp.ones((wide, 128), jnp.bfloat16)], axis=1)
            accum += jnp.dot(p, v, preferred_element_type=jnp.float32)
        here = slice(j * sub, (j + 1) * sub)
        out_ref[here] = gate_ref[here, 1:2] * (accum[:, :128] / accum[:, 128:])

    tops = [score(0)]
    for j in range(blocks):
        if j + 1 < blocks:
            tops.append(score(j + 1))
        mix(j, tops[j])


def window_branch(who, q, four, two, one, paired, gates, scale, heads, block=1024, sub=256):
    total = q.shape[0]

    def row(width):
        return pl.BlockSpec((block, width), lambda i, w: (i, 0))

    def whole(array):
        return pl.BlockSpec(array.shape, lambda i, w: (0, 0))

    return pl.pallas_call(
        functools.partial(window_kernel, scale, heads),
        grid_spec=pltpu.PrefetchScalarGridSpec(
            num_scalar_prefetch=1,
            grid=(total // block,),
            in_specs=[
                row(q.shape[1]),
                whole(four),
                whole(two),
                whole(one),
                whole(paired),
                row(2),
            ],
            out_specs=row(128),
            scratch_shapes=[pltpu.VMEM((sub, 640), jnp.float32)] * 2,
        ),
        out_shape=jax.ShapeDtypeStruct((total, 128), jnp.float32),
        compiler_params=pltpu.CompilerParams(vmem_limit_bytes=GRANT),
        name="window",
        cost_estimate=pl.CostEstimate(
            flops=2 * total * 640 * 512, bytes_accessed=4000000, transcendentals=total * 640
        ),
    )(who, q, four, two, one, paired, gates)


def far_scores(heads, device, core, q, kv_ref, s_ref, base):
    block = q.shape[0]
    zeros = jnp.zeros((block, 64), q.dtype)
    queries = (
        jnp.concatenate([q, zeros], axis=1),
        jnp.concatenate([q[:, :128], zeros, q[:, 128:]], axis=1),
    )
    token = base + lax.broadcasted_iota(jnp.int32, (block, 256), 0) // heads
    lane = lax.broadcasted_iota(jnp.int32, (1, 256), 1)
    top = None
    for g in range(kv_ref.shape[0] // 4):
        for half in range(2):
            low = kv_ref[4 * g : 4 * g + 4, 64 * half : 64 * half + 64].reshape(256, 128)
            high = kv_ref[4 * g : 4 * g + 4, 128:192].reshape(256, 128)
            s = nt(queries[half], jnp.concatenate([low, high], axis=1))
            z = 8 * half + (lane % 64) // 8
            owner = (2 * z + core) * 16 + 4 * g + lane // 64
            end = (owner - device) * 128 + STRIDE * (lane % 8) + STRIDE - 1
            s = jnp.where(end <= token, s, LOW)
            slot = 2 * g + half
            s_ref[:, 256 * slot : 256 * slot + 256] = s
            most = jnp.maximum(s[:, :128], s[:, 128:])
            top = most if top is None else jnp.maximum(top, most)
    return jnp.maximum(jnp.max(top, axis=1, keepdims=True), FLOOR)


def far_mix(scale, s_ref, top, kv_ref):
    ones = jnp.ones((256, 128), jnp.bfloat16)
    accum = jnp.zeros((s_ref.shape[0], 256), jnp.float32)
    for g in range(kv_ref.shape[0] // 4):
        for half in range(2):
            slot = 2 * g + half
            s = s_ref[:, 256 * slot : 256 * slot + 256]
            p = jnp.exp2((s - top) * (scale * LOG2E)).astype(jnp.bfloat16)
            v = kv_ref[4 * g : 4 * g + 4, 192 + 64 * half : 256 + 64 * half].reshape(256, 128)
            accum += jnp.dot(
                p, jnp.concatenate([v, ones], axis=1), preferred_element_type=jnp.float32
            )
    return accum


def skewed(scale, heads, device, core, q_ref, kv_ref, scratch, finish):
    sub = scratch[0].shape[0]
    blocks = q_ref.shape[0] // sub
    base = pl.program_id(0) * (q_ref.shape[0] // heads)

    def score(j):
        return far_scores(
            heads,
            device,
            core,
            q_ref[j * sub : (j + 1) * sub],
            kv_ref,
            scratch[j % 2],
            base + j * (sub // heads),
        )

    tops = [score(0)]
    for j in range(blocks):
        if j + 1 < blocks:
            tops.append(score(j + 1))
        finish(slice(j * sub, (j + 1) * sub), far_mix(scale, scratch[j % 2], tops[j], kv_ref), tops[j])


def first_kernel(scale, heads, who, q_ref, kv_ref, acc_ref, top_ref, *scratch):
    def finish(here, accum, top):
        acc_ref[here] = accum
        top_ref[here] = jnp.broadcast_to(top, (accum.shape[0], 128))

    skewed(scale, heads, who[0], who[1], q_ref, kv_ref, scratch, finish)


def second_kernel(
    scale, heads, who, q_ref, kv_ref, acc_ref, top_ref, win_ref, gate_ref, out_ref, *scratch
):
    def finish(here, accum, top):
        other = top_ref[here]
        most = jnp.maximum(other, top)
        grow = jnp.exp2((other - most) * (scale * LOG2E))
        shrink = jnp.exp2((top - most) * (scale * LOG2E))
        number = acc_ref[here, :128] * grow + accum[:, :128] * shrink
        total = acc_ref[here, 128:] * grow + accum[:, 128:] * shrink
        present = total > 0.0
        compressed = jnp.where(present, number / jnp.where(present, total, 1.0), 0.0)
        out_ref[here] = (gate_ref[here, 0:1] * compressed + win_ref[here]).astype(out_ref.dtype)

    skewed(scale, heads, who[0], 1 - who[1], q_ref, kv_ref, scratch, finish)


def first_half(who, q, kv, scale, heads, block=2048, sub=256):
    total = q.shape[0]
    keys = kv.shape[0] * 128
    return pl.pallas_call(
        functools.partial(first_kernel, scale, heads),
        grid_spec=pltpu.PrefetchScalarGridSpec(
            num_scalar_prefetch=1,
            grid=(total // block,),
            in_specs=[
                pl.BlockSpec((block, q.shape[1]), lambda i, w: (i, 0)),
                pl.BlockSpec(memory_space=pltpu.VMEM),
            ],
            out_specs=[
                pl.BlockSpec((block, 256), lambda i, w: (i, 0)),
                pl.BlockSpec((block, 128), lambda i, w: (i, 0)),
            ],
            scratch_shapes=[pltpu.VMEM((sub, keys), jnp.float32)] * 2,
        ),
        out_shape=[
            jax.ShapeDtypeStruct((total, 256), jnp.float32),
            jax.ShapeDtypeStruct((total, 128), jnp.float32),
        ],
        compiler_params=pltpu.CompilerParams(vmem_limit_bytes=GRANT),
        name="first_half",
        cost_estimate=pl.CostEstimate(
            flops=2 * total * keys * 512, bytes_accessed=3000000, transcendentals=total * keys
        ),
    )(who, q, kv)


def second_half(who, q, kv, acc, top, win, gates, scale, heads, block=2048, sub=256):
    total = q.shape[0]
    keys = kv.shape[0] * 128

    def row(width):
        return pl.BlockSpec((block, width), lambda i, w: (i, 0))

    return pl.pallas_call(
        functools.partial(second_kernel, scale, heads),
        grid_spec=pltpu.PrefetchScalarGridSpec(
            num_scalar_prefetch=1,
            grid=(total // block,),
            in_specs=[
                row(q.shape[1]),
                pl.BlockSpec(memory_space=pltpu.VMEM),
                row(256),
                row(128),
                row(128),
                row(2),
            ],
            out_specs=row(128),
            scratch_shapes=[pltpu.VMEM((sub, keys), jnp.float32)] * 2,
        ),
        out_shape=jax.ShapeDtypeStruct((total, 128), jnp.bfloat16),
        compiler_params=pltpu.CompilerParams(vmem_limit_bytes=GRANT),
        name="second_half",
        cost_estimate=pl.CostEstimate(
            flops=2 * total * keys * 512, bytes_accessed=5000000, transcendentals=total * keys
        ),
    )(who, q, kv, acc, top, win, gates)


def local(
    queries, keys, values, key_first, key_second, value_first, value_second, gate_table, gate_index
):
    rows, heads, depth = queries.shape
    outer, inner = lax.axis_index("sa"), lax.axis_index("sb")
    core = outer % 2
    device = outer * lax.axis_size("sb") + inner
    who = jnp.stack([device, core]).astype(jnp.int32)
    planes = lax.axis_size("sa") // 2
    scale = depth ** (-0.5)
    paired = pair(keys, values)
    one = shifted(paired, ("sa", "sb"), 1)
    kfirst = key_first.T
    hidden = own_blocks(paired, kfirst, value_first)
    payload = summary(one, hidden, kfirst, key_second, value_first, value_second, planes)
    payload, later, again = lax.optimization_barrier((payload, one, paired))
    groups = [[2 * z + c for z in range(planes)] for c in range(2)]
    column = lax.all_to_all(payload, "sa", 0, 0, axis_index_groups=groups)
    four = shifted(again, ("sa", "sb"), 4)
    two = shifted(jnp.concatenate([later, again], axis=0), ("sa", "sb"), 2)
    query_rows = queries.reshape(rows * heads, depth)
    chosen = gate_index.reshape(rows * heads)
    onehot = (chosen[:, None] == lax.iota(jnp.int32, gate_table.shape[0])[None, :]).astype(
        jnp.float32
    )
    gates = jnp.sum(onehot[:, :, None] * gate_table[None, :, :], axis=1)
    copies = pack(column, lax.axis_size("sb"))
    mine = lax.all_to_all(copies, "sb", 0, 0)
    win = window_branch(who, query_rows, four, two, later, again, gates, scale, heads)
    mine, win = lax.optimization_barrier((mine, win))
    other = lax.ppermute(mine, "sa", [(i, i ^ 1) for i in range(2 * planes)])
    acc, top = first_half(who, query_rows, mine, scale, heads)
    mixed = second_half(who, query_rows, other, acc, top, win, gates, scale, heads)
    return mixed.reshape(rows, heads, values.shape[1])


def solution(mesh):
    in_specs = (
        P(("sa", "sb"), None, None),
        P(("sa", "sb"), None),
        P(("sa", "sb"), None),
        P(),
        P(),
        P(),
        P(),
        P(),
        P(("sa", "sb"), None),
    )
    out_specs = P(("sa", "sb"), None, None)
    return jax.shard_map(local, mesh=mesh, in_specs=in_specs, out_specs=out_specs, check_vma=False)
```

```python
import functools

import jax
import jax.numpy as jnp
from jax import lax
from jax.experimental import pallas as pl
from jax.experimental.pallas import tpu as pltpu
from jax.sharding import PartitionSpec as P


STRIDE = 16
LOG2E = 1.4426950408889634
LOW = -1e30
FLOOR = -1e29
GRANT = 20 << 20


def nt(a, b):
    return lax.dot_general(a, b, (((1,), (1,)), ((), ())), preferred_element_type=jnp.float32)


def shifted(shard, axis, by):
    size = lax.axis_size(axis)
    pairs = [(i, i + by) for i in range(size) if 0 <= i + by < size]
    return lax.ppermute(shard, axis, pairs)


def pair_kernel(keys_ref, values_ref, out_ref):
    out_ref[:, :192] = keys_ref[...].astype(jnp.float32).T.astype(out_ref.dtype)
    out_ref[:, 192:256] = jnp.zeros((out_ref.shape[0], 64), out_ref.dtype)
    out_ref[:, 256:] = values_ref[...]


def pair(keys, values):
    return pl.pallas_call(
        pair_kernel,
        in_specs=[pl.BlockSpec(memory_space=pltpu.VMEM)] * 2,
        out_specs=pl.BlockSpec(memory_space=pltpu.VMEM),
        out_shape=jax.ShapeDtypeStruct((keys.shape[0], 384), keys.dtype),
        compiler_params=pltpu.CompilerParams(vmem_limit_bytes=GRANT),
        name="pair",
    )(keys.T, values)


def silu(x):
    return x * (1.0 / (1.0 + jnp.exp(-x)))


def segments(wide_ref, count):
    keys, values = [], []
    for first in range(STRIDE):
        some = [wide_ref[part, pl.ds(first, count, stride=STRIDE), :] for part in range(3)]
        keys.append(jnp.concatenate([some[0], some[1][:, :64]], axis=1))
        values.append(some[2])
    keys = jnp.concatenate(keys, axis=1).astype(jnp.bfloat16)
    values = jnp.concatenate(values, axis=1).astype(jnp.bfloat16)
    return keys, values


def own_kernel(pair_ref, kfirst_ref, vfirst_ref, hidden_ref, wide):
    half_keys = kfirst_ref.shape[1] // 2
    half_values = vfirst_ref.shape[0] // 2
    count = pair_ref.shape[0] // STRIDE
    for part in range(3):
        lanes = slice(128 * part, 128 * part + 128)
        wide[part] = pair_ref[:, lanes].astype(jnp.float32)
    keys, values = segments(wide, count)
    nothing = jnp.zeros((count, 64), jnp.float32)
    back = jnp.concatenate(
        [
            nt(keys, kfirst_ref[:, half_keys:]),
            nothing,
            jnp.dot(values, vfirst_ref[half_values:], preferred_element_type=jnp.float32),
        ],
        axis=1,
    )
    ahead = jnp.concatenate(
        [
            nt(keys, kfirst_ref[:, :half_keys]),
            nothing,
            jnp.dot(values, vfirst_ref[:half_values], preferred_element_type=jnp.float32),
        ],
        axis=1,
    )
    row = lax.broadcasted_iota(jnp.int32, back.shape, 0)
    hidden_ref[...] = back + jnp.where(row == 0, 0.0, pltpu.roll(ahead, 1, 0))


def own_blocks(paired, kfirst, vfirst):
    rows = paired.shape[0]
    inside = pl.BlockSpec(memory_space=pltpu.VMEM)
    return pl.pallas_call(
        own_kernel,
        in_specs=[inside] * 3,
        out_specs=inside,
        out_shape=jax.ShapeDtypeStruct((rows // STRIDE, 384), jnp.float32),
        scratch_shapes=[pltpu.VMEM((3, rows, 128), jnp.float32)],
        compiler_params=pltpu.CompilerParams(vmem_limit_bytes=GRANT),
        name="own_blocks",
        cost_estimate=pl.CostEstimate(
            flops=1000000000, bytes_accessed=8000000, transcendentals=0
        ),
    )(paired, kfirst, vfirst)


def summary_kernel(
    before_ref, hidden_ref, kfirst_ref, ksecond_ref, vfirst_ref, vsecond_ref, out_ref, wide
):
    rows = before_ref.shape[0]
    count = hidden_ref.shape[0]
    for part in range(3):
        lanes = slice(128 * part, 128 * part + 128)
        wide[part] = before_ref[:, lanes].astype(jnp.float32)
    keys, values = segments(wide, rows // STRIDE)
    ahead = jnp.concatenate(
        [
            nt(keys, kfirst_ref[:, : kfirst_ref.shape[1] // 2]),
            jnp.zeros((count, 64), jnp.float32),
            jnp.dot(
                values,
                vfirst_ref[: vfirst_ref.shape[0] // 2],
                preferred_element_type=jnp.float32,
            ),
        ],
        axis=1,
    )
    row = lax.broadcasted_iota(jnp.int32, ahead.shape, 0)
    hidden = hidden_ref[...] + jnp.where(row == 0, pltpu.roll(ahead, 1, 0), 0.0)
    hidden = silu(hidden).astype(jnp.bfloat16)
    key = jnp.dot(hidden[:, :192], ksecond_ref[...], preferred_element_type=jnp.float32)
    value = jnp.dot(hidden[:, 256:], vsecond_ref[...], preferred_element_type=jnp.float32)
    high = jnp.concatenate([key[:, 128:], jnp.zeros((count, 64), jnp.float32)], axis=1)
    payload = jnp.concatenate([key[:, :128], high, value], axis=0).astype(out_ref.dtype)
    for copy in range(out_ref.shape[0]):
        out_ref[copy] = payload


def summary(before, hidden, kfirst, key_second, vfirst, value_second, copies):
    inside = pl.BlockSpec(memory_space=pltpu.VMEM)
    default = pl.BlockSpec()
    return pl.pallas_call(
        summary_kernel,
        in_specs=[inside, inside, inside, default, inside, default],
        out_specs=inside,
        out_shape=jax.ShapeDtypeStruct((copies, 3 * hidden.shape[0], 128), jnp.bfloat16),
        scratch_shapes=[pltpu.VMEM((3,) + (before.shape[0], 128), jnp.float32)],
        compiler_params=pltpu.CompilerParams(vmem_limit_bytes=GRANT),
        name="summary",
    )(before, hidden, kfirst, key_second, vfirst, value_second)


def pack_kernel(column_ref, out_ref):
    planes = column_ref.shape[0]
    half = planes // 2
    count = column_ref.shape[1] // 3
    low = column_ref[:, :count].astype(jnp.float32).reshape(planes * count, 128)
    high = column_ref[:, count : 2 * count].astype(jnp.float32)
    high = jnp.concatenate(
        [
            high[:half].reshape(half * count, 128)[:, :64],
            high[half:].reshape(half * count, 128)[:, :64],
        ],
        axis=1,
    )
    value = column_ref[:, 2 * count :].astype(jnp.float32).reshape(planes * count, 128)
    packed = jnp.concatenate([low, high, value], axis=0).astype(out_ref.dtype)
    for copy in range(out_ref.shape[0]):
        out_ref[copy] = packed


def pack(column, copies):
    planes, rows, lanes = column.shape
    inside = pl.BlockSpec(memory_space=pltpu.VMEM)
    return pl.pallas_call(
        pack_kernel,
        in_specs=[inside],
        out_specs=inside,
        out_shape=jax.ShapeDtypeStruct((copies, planes * rows * 5 // 6, lanes), column.dtype),
        compiler_params=pltpu.CompilerParams(vmem_limit_bytes=GRANT),
        name="pack",
    )(column)


def window_kernel(
    scale, heads, who, q_ref, four_ref, two_ref, one_ref, pair_ref, gate_ref, out_ref, *scratch
):
    sub = scratch[0].shape[0]
    size = pair_ref.shape[0]
    blocks = q_ref.shape[0] // sub
    device = who[0]
    base = pl.program_id(0) * (q_ref.shape[0] // heads)
    near = (
        jnp.concatenate([four_ref[...], two_ref[:size]], axis=0),
        jnp.concatenate([two_ref[size:], one_ref[...]], axis=0),
        pair_ref[...],
    )
    begins = [
        size * jnp.clip(4 - device, 0, 2),
        size * jnp.clip(2 - device, 0, 2),
    ]

    def score(j):
        s_ref = scratch[j % 2]
        q = q_ref[j * sub : (j + 1) * sub]
        q = jnp.concatenate([q, jnp.zeros((sub, 64), q.dtype)], axis=1)
        token = base + j * (sub // heads) + lax.broadcasted_iota(jnp.int32, (sub, 256), 0) // heads
        lane = lax.broadcasted_iota(jnp.int32, (sub, 256), 1)
        s0 = nt(q, near[0][:, :256])
        s0 = jnp.where(lane > jnp.maximum(token, begins[0] - 1), s0, LOW)
        s1 = nt(q, near[1][:, :256])
        s1 = jnp.where(lane >= begins[1], s1, LOW)
        s2 = nt(q, near[2][:, :256])
        s2 = jnp.where(lane[:, :128] <= token[:, :128], s2, LOW)
        s_ref[:, :256] = s0
        s_ref[:, 256:512] = s1
        s_ref[:, 512:] = s2
        top = jnp.maximum(jnp.maximum(s0, s1), jnp.concatenate([s2, s2], axis=1))
        return jnp.maximum(jnp.max(top, axis=1, keepdims=True), FLOOR)

    def mix(j, top):
        s_ref = scratch[j % 2]
        accum = jnp.zeros((sub, 256), jnp.float32)
        for part, at in enumerate((0, 256, 512)):
            wide = near[part].shape[0]
            p = jnp.exp2((s_ref[:, at : at + wide] - top) * (scale * LOG2E)).astype(jnp.bfloat16)
            v = jnp.concatenate([near[part][:, 256:], jnp.ones((wide, 128), jnp.bfloat16)], axis=1)
            accum += jnp.dot(p, v, preferred_element_type=jnp.float32)
        here = slice(j * sub, (j + 1) * sub)
        out_ref[here] = gate_ref[here, 1:2] * (accum[:, :128] / accum[:, 128:])

    tops = [score(0)]
    for j in range(blocks):
        if j + 1 < blocks:
            tops.append(score(j + 1))
        mix(j, tops[j])


def window_branch(who, q, four, two, one, paired, gates, scale, heads, block=1024, sub=256):
    total = q.shape[0]

    def row(width):
        return pl.BlockSpec((block, width), lambda i, w: (i, 0))

    def whole(array):
        return pl.BlockSpec(array.shape, lambda i, w: (0, 0))

    return pl.pallas_call(
        functools.partial(window_kernel, scale, heads),
        grid_spec=pltpu.PrefetchScalarGridSpec(
            num_scalar_prefetch=1,
            grid=(total // block,),
            in_specs=[
                row(q.shape[1]),
                whole(four),
                whole(two),
                whole(one),
                whole(paired),
                row(2),
            ],
            out_specs=row(128),
            scratch_shapes=[pltpu.VMEM((sub, 640), jnp.float32)] * 2,
        ),
        out_shape=jax.ShapeDtypeStruct((total, 128), jnp.float32),
        compiler_params=pltpu.CompilerParams(vmem_limit_bytes=GRANT),
        name="window",
        cost_estimate=pl.CostEstimate(
            flops=2 * total * 640 * 512, bytes_accessed=4000000, transcendentals=total * 640
        ),
    )(who, q, four, two, one, paired, gates)


def far_scores(heads, device, core, q, kv_ref, s_ref, base, quarters):
    block = q.shape[0]
    zeros = jnp.zeros((block, 64), q.dtype)
    queries = (
        jnp.concatenate([q, zeros], axis=1),
        jnp.concatenate([q[:, :128], zeros, q[:, 128:]], axis=1),
    )
    token = base + lax.broadcasted_iota(jnp.int32, (block, 256), 0) // heads
    lane = lax.broadcasted_iota(jnp.int32, (1, 256), 1)
    top = None
    for quarter in range(quarters):
        for g in range(kv_ref.shape[0] // 8):
            some = slice(8 * g, 8 * g + 8)
            begin = 32 * quarter
            low = kv_ref[some, begin : begin + 32].reshape(256, 128)
            begin = 128 + 32 * (quarter % 2)
            high = kv_ref[some, begin : begin + 32].reshape(256, 128)
            s = nt(queries[quarter // 2], jnp.concatenate([low, high], axis=1))
            z = 4 * quarter + (lane % 32) // 8
            owner = (2 * z + core) * 16 + 8 * g + lane // 32
            end = (owner - device) * 128 + STRIDE * (lane % 8) + STRIDE - 1
            s = jnp.where(end <= token, s, LOW)
            slot = 2 * quarter + g
            s_ref[:, 256 * slot : 256 * slot + 256] = s
            most = jnp.maximum(s[:, :128], s[:, 128:])
            top = most if top is None else jnp.maximum(top, most)
    return jnp.maximum(jnp.max(top, axis=1, keepdims=True), FLOOR)


def far_mix(scale, s_ref, top, kv_ref, quarters):
    ones = jnp.ones((256, 128), jnp.bfloat16)
    accum = jnp.zeros((s_ref.shape[0], 256), jnp.float32)
    for quarter in range(quarters):
        for g in range(kv_ref.shape[0] // 8):
            slot = 2 * quarter + g
            s = s_ref[:, 256 * slot : 256 * slot + 256]
            p = jnp.exp2((s - top) * (scale * LOG2E)).astype(jnp.bfloat16)
            begin = 192 + 32 * quarter
            v = kv_ref[8 * g : 8 * g + 8, begin : begin + 32].reshape(256, 128)
            accum += jnp.dot(
                p, jnp.concatenate([v, ones], axis=1), preferred_element_type=jnp.float32
            )
    return accum


def skewed(scale, heads, who, core, q_ref, kv_ref, scratch, finish):
    sub = scratch[0].shape[0]
    blocks = q_ref.shape[0] // sub
    base = pl.program_id(0) * (q_ref.shape[0] // heads)
    plane = who[2]

    def run(quarters):
        def score(j):
            return far_scores(
                heads,
                who[0],
                core,
                q_ref[j * sub : (j + 1) * sub],
                kv_ref,
                scratch[j % 2],
                base + j * (sub // heads),
                quarters,
            )

        tops = [score(0)]
        for j in range(blocks):
            if j + 1 < blocks:
                tops.append(score(j + 1))
            mix = far_mix(scale, scratch[j % 2], tops[j], kv_ref, quarters)
            finish(slice(j * sub, (j + 1) * sub), mix, tops[j])

    @pl.when(plane < 4)
    def _():
        run(1)

    @pl.when((plane >= 4) & (plane < 8))
    def _():
        run(2)

    @pl.when(plane >= 8)
    def _():
        run(4)


def first_kernel(scale, heads, who, q_ref, kv_ref, acc_ref, top_ref, *scratch):
    def finish(here, accum, top):
        acc_ref[here] = accum
        top_ref[here] = jnp.broadcast_to(top, (accum.shape[0], 128))

    skewed(scale, heads, who, who[1], q_ref, kv_ref, scratch, finish)


def second_kernel(
    scale, heads, who, q_ref, kv_ref, acc_ref, top_ref, win_ref, gate_ref, out_ref, *scratch
):
    def finish(here, accum, top):
        other = top_ref[here]
        most = jnp.maximum(other, top)
        grow = jnp.exp2((other - most) * (scale * LOG2E))
        shrink = jnp.exp2((top - most) * (scale * LOG2E))
        number = acc_ref[here, :128] * grow + accum[:, :128] * shrink
        total = acc_ref[here, 128:] * grow + accum[:, 128:] * shrink
        present = total > 0.0
        compressed = jnp.where(present, number / jnp.where(present, total, 1.0), 0.0)
        out_ref[here] = (gate_ref[here, 0:1] * compressed + win_ref[here]).astype(out_ref.dtype)

    skewed(scale, heads, who, 1 - who[1], q_ref, kv_ref, scratch, finish)


def first_half(who, q, kv, scale, heads, block=2048, sub=256):
    total = q.shape[0]
    keys = kv.shape[0] * 128
    return pl.pallas_call(
        functools.partial(first_kernel, scale, heads),
        grid_spec=pltpu.PrefetchScalarGridSpec(
            num_scalar_prefetch=1,
            grid=(total // block,),
            in_specs=[
                pl.BlockSpec((block, q.shape[1]), lambda i, w: (i, 0)),
                pl.BlockSpec(memory_space=pltpu.VMEM),
            ],
            out_specs=[
                pl.BlockSpec((block, 256), lambda i, w: (i, 0)),
                pl.BlockSpec((block, 128), lambda i, w: (i, 0)),
            ],
            scratch_shapes=[pltpu.VMEM((sub, keys), jnp.float32)] * 2,
        ),
        out_shape=[
            jax.ShapeDtypeStruct((total, 256), jnp.float32),
            jax.ShapeDtypeStruct((total, 128), jnp.float32),
        ],
        compiler_params=pltpu.CompilerParams(vmem_limit_bytes=GRANT),
        name="first_half",
        cost_estimate=pl.CostEstimate(
            flops=2 * total * keys * 512, bytes_accessed=3000000, transcendentals=total * keys
        ),
    )(who, q, kv)


def second_half(who, q, kv, acc, top, win, gates, scale, heads, block=2048, sub=256):
    total = q.shape[0]
    keys = kv.shape[0] * 128

    def row(width):
        return pl.BlockSpec((block, width), lambda i, w: (i, 0))

    return pl.pallas_call(
        functools.partial(second_kernel, scale, heads),
        grid_spec=pltpu.PrefetchScalarGridSpec(
            num_scalar_prefetch=1,
            grid=(total // block,),
            in_specs=[
                row(q.shape[1]),
                pl.BlockSpec(memory_space=pltpu.VMEM),
                row(256),
                row(128),
                row(128),
                row(2),
            ],
            out_specs=row(128),
            scratch_shapes=[pltpu.VMEM((sub, keys), jnp.float32)] * 2,
        ),
        out_shape=jax.ShapeDtypeStruct((total, 128), jnp.bfloat16),
        compiler_params=pltpu.CompilerParams(vmem_limit_bytes=GRANT),
        name="second_half",
        cost_estimate=pl.CostEstimate(
            flops=2 * total * keys * 512, bytes_accessed=5000000, transcendentals=total * keys
        ),
    )(who, q, kv, acc, top, win, gates)


def local(
    queries, keys, values, key_first, key_second, value_first, value_second, gate_table, gate_index
):
    rows, heads, depth = queries.shape
    outer, inner = lax.axis_index("sa"), lax.axis_index("sb")
    core = outer % 2
    device = outer * lax.axis_size("sb") + inner
    who = jnp.stack([device, core, outer // 2]).astype(jnp.int32)
    planes = lax.axis_size("sa") // 2
    scale = depth ** (-0.5)
    paired = pair(keys, values)
    one = shifted(paired, ("sa", "sb"), 1)
    kfirst = key_first.T
    hidden = own_blocks(paired, kfirst, value_first)
    payload = summary(one, hidden, kfirst, key_second, value_first, value_second, planes)
    payload, later, again = lax.optimization_barrier((payload, one, paired))
    groups = [[2 * z + c for z in range(planes)] for c in range(2)]
    column = lax.all_to_all(payload, "sa", 0, 0, axis_index_groups=groups)
    four = shifted(again, ("sa", "sb"), 4)
    two = shifted(jnp.concatenate([later, again], axis=0), ("sa", "sb"), 2)
    query_rows = queries.reshape(rows * heads, depth)
    chosen = gate_index.reshape(rows * heads)
    onehot = (chosen[:, None] == lax.iota(jnp.int32, gate_table.shape[0])[None, :]).astype(
        jnp.float32
    )
    gates = jnp.sum(onehot[:, :, None] * gate_table[None, :, :], axis=1)
    copies = pack(column, lax.axis_size("sb"))
    mine = lax.all_to_all(copies, "sb", 0, 0)
    win = window_branch(who, query_rows, four, two, later, again, gates, scale, heads)
    mine, win = lax.optimization_barrier((mine, win))
    other = lax.ppermute(mine, "sa", [(i, i ^ 1) for i in range(2 * planes)])
    acc, top = first_half(who, query_rows, mine, scale, heads)
    mixed = second_half(who, query_rows, other, acc, top, win, gates, scale, heads)
    return mixed.reshape(rows, heads, values.shape[1])


def solution(mesh):
    in_specs = (
        P(("sa", "sb"), None, None),
        P(("sa", "sb"), None),
        P(("sa", "sb"), None),
        P(),
        P(),
        P(),
        P(),
        P(),
        P(("sa", "sb"), None),
    )
    out_specs = P(("sa", "sb"), None, None)
    return jax.shard_map(local, mesh=mesh, in_specs=in_specs, out_specs=out_specs, check_vma=False)
```

```python
import functools

import jax
import jax.numpy as jnp
from jax import lax
from jax.experimental import pallas as pl
from jax.experimental.pallas import tpu as pltpu
from jax.sharding import PartitionSpec as P


STRIDE = 16
LOG2E = 1.4426950408889634
LOW = -1e30
FLOOR = -1e29
GRANT = 20 << 20


def nt(a, b):
    return lax.dot_general(a, b, (((1,), (1,)), ((), ())), preferred_element_type=jnp.float32)


def shifted(shard, axis, by):
    size = lax.axis_size(axis)
    pairs = [(i, i + by) for i in range(size) if 0 <= i + by < size]
    return lax.ppermute(shard, axis, pairs)


def pair_kernel(keys_ref, values_ref, out_ref):
    out_ref[:, :192] = keys_ref[...].astype(jnp.float32).T.astype(out_ref.dtype)
    out_ref[:, 192:256] = jnp.zeros((out_ref.shape[0], 64), out_ref.dtype)
    out_ref[:, 256:] = values_ref[...]


def pair(keys, values):
    return pl.pallas_call(
        pair_kernel,
        in_specs=[pl.BlockSpec(memory_space=pltpu.VMEM)] * 2,
        out_specs=pl.BlockSpec(memory_space=pltpu.VMEM),
        out_shape=jax.ShapeDtypeStruct((keys.shape[0], 384), keys.dtype),
        compiler_params=pltpu.CompilerParams(vmem_limit_bytes=GRANT),
        name="pair",
    )(keys.T, values)


def silu(x):
    return x * (1.0 / (1.0 + jnp.exp(-x)))


def segments(wide_ref, count):
    keys, values = [], []
    for first in range(STRIDE):
        some = [wide_ref[part, pl.ds(first, count, stride=STRIDE), :] for part in range(3)]
        keys.append(jnp.concatenate([some[0], some[1][:, :64]], axis=1))
        values.append(some[2])
    keys = jnp.concatenate(keys, axis=1).astype(jnp.bfloat16)
    values = jnp.concatenate(values, axis=1).astype(jnp.bfloat16)
    return keys, values


def own_kernel(pair_ref, kfirst_ref, vfirst_ref, hidden_ref, wide):
    half_keys = kfirst_ref.shape[1] // 2
    half_values = vfirst_ref.shape[0] // 2
    count = pair_ref.shape[0] // STRIDE
    for part in range(3):
        lanes = slice(128 * part, 128 * part + 128)
        wide[part] = pair_ref[:, lanes].astype(jnp.float32)
    keys, values = segments(wide, count)
    nothing = jnp.zeros((count, 64), jnp.float32)
    back = jnp.concatenate(
        [
            nt(keys, kfirst_ref[:, half_keys:]),
            nothing,
            jnp.dot(values, vfirst_ref[half_values:], preferred_element_type=jnp.float32),
        ],
        axis=1,
    )
    ahead = jnp.concatenate(
        [
            nt(keys, kfirst_ref[:, :half_keys]),
            nothing,
            jnp.dot(values, vfirst_ref[:half_values], preferred_element_type=jnp.float32),
        ],
        axis=1,
    )
    row = lax.broadcasted_iota(jnp.int32, back.shape, 0)
    hidden_ref[...] = back + jnp.where(row == 0, 0.0, pltpu.roll(ahead, 1, 0))


def own_blocks(paired, kfirst, vfirst):
    rows = paired.shape[0]
    inside = pl.BlockSpec(memory_space=pltpu.VMEM)
    return pl.pallas_call(
        own_kernel,
        in_specs=[inside] * 3,
        out_specs=inside,
        out_shape=jax.ShapeDtypeStruct((rows // STRIDE, 384), jnp.float32),
        scratch_shapes=[pltpu.VMEM((3, rows, 128), jnp.float32)],
        compiler_params=pltpu.CompilerParams(vmem_limit_bytes=GRANT),
        name="own_blocks",
        cost_estimate=pl.CostEstimate(
            flops=1000000000, bytes_accessed=8000000, transcendentals=0
        ),
    )(paired, kfirst, vfirst)


def summary_kernel(
    before_ref, hidden_ref, kfirst_ref, ksecond_ref, vfirst_ref, vsecond_ref, out_ref, wide
):
    rows = before_ref.shape[0]
    count = hidden_ref.shape[0]
    for part in range(3):
        lanes = slice(128 * part, 128 * part + 128)
        wide[part] = before_ref[:, lanes].astype(jnp.float32)
    keys, values = segments(wide, rows // STRIDE)
    ahead = jnp.concatenate(
        [
            nt(keys, kfirst_ref[:, : kfirst_ref.shape[1] // 2]),
            jnp.zeros((count, 64), jnp.float32),
            jnp.dot(
                values,
                vfirst_ref[: vfirst_ref.shape[0] // 2],
                preferred_element_type=jnp.float32,
            ),
        ],
        axis=1,
    )
    row = lax.broadcasted_iota(jnp.int32, ahead.shape, 0)
    hidden = hidden_ref[...] + jnp.where(row == 0, pltpu.roll(ahead, 1, 0), 0.0)
    hidden = silu(hidden).astype(jnp.bfloat16)
    key = jnp.dot(hidden[:, :192], ksecond_ref[...], preferred_element_type=jnp.float32)
    value = jnp.dot(hidden[:, 256:], vsecond_ref[...], preferred_element_type=jnp.float32)
    high = jnp.concatenate([key[:, 128:], jnp.zeros((count, 64), jnp.float32)], axis=1)
    payload = jnp.concatenate([key[:, :128], high, value], axis=0).astype(out_ref.dtype)
    for copy in range(out_ref.shape[0]):
        out_ref[copy] = payload


def summary(before, hidden, kfirst, key_second, vfirst, value_second, copies):
    inside = pl.BlockSpec(memory_space=pltpu.VMEM)
    default = pl.BlockSpec()
    return pl.pallas_call(
        summary_kernel,
        in_specs=[inside, inside, inside, default, inside, default],
        out_specs=inside,
        out_shape=jax.ShapeDtypeStruct((copies, 3 * hidden.shape[0], 128), jnp.bfloat16),
        scratch_shapes=[pltpu.VMEM((3,) + (before.shape[0], 128), jnp.float32)],
        compiler_params=pltpu.CompilerParams(vmem_limit_bytes=GRANT),
        name="summary",
    )(before, hidden, kfirst, key_second, vfirst, value_second)


def pack_kernel(column_ref, out_hbm, packed, sems):
    planes = column_ref.shape[0]
    half = planes // 2
    count = column_ref.shape[1] // 3
    low = column_ref[:, :count].astype(jnp.float32).reshape(planes * count, 128)
    high = column_ref[:, count : 2 * count].astype(jnp.float32)
    high = jnp.concatenate(
        [
            high[:half].reshape(half * count, 128)[:, :64],
            high[half:].reshape(half * count, 128)[:, :64],
        ],
        axis=1,
    )
    value = column_ref[:, 2 * count :].astype(jnp.float32).reshape(planes * count, 128)
    packed[...] = jnp.concatenate([low, high, value], axis=0).astype(packed.dtype)
    moves = [
        pltpu.make_async_copy(packed, out_hbm.at[copy], sems.at[copy])
        for copy in range(out_hbm.shape[0])
    ]
    for move in moves:
        move.start()
    for move in moves:
        move.wait()


def pack(column, copies):
    planes, rows, lanes = column.shape
    size = planes * rows * 5 // 6
    return pl.pallas_call(
        pack_kernel,
        in_specs=[pl.BlockSpec(memory_space=pltpu.VMEM)],
        out_specs=pl.BlockSpec(memory_space=pl.ANY),
        out_shape=jax.ShapeDtypeStruct((copies, size, lanes), column.dtype),
        scratch_shapes=[
            pltpu.VMEM((size, lanes), column.dtype),
            pltpu.SemaphoreType.DMA((copies,)),
        ],
        compiler_params=pltpu.CompilerParams(vmem_limit_bytes=GRANT),
        name="pack",
    )(column)


def window_kernel(
    scale, heads, who, q_ref, four_ref, two_ref, one_ref, pair_ref, gate_ref, out_ref, *scratch
):
    sub = scratch[0].shape[0]
    size = pair_ref.shape[0]
    blocks = q_ref.shape[0] // sub
    device = who[0]
    base = pl.program_id(0) * (q_ref.shape[0] // heads)
    near = (
        jnp.concatenate([four_ref[...], two_ref[:size]], axis=0),
        jnp.concatenate([two_ref[size:], one_ref[...]], axis=0),
        pair_ref[...],
    )
    begins = [
        size * jnp.clip(4 - device, 0, 2),
        size * jnp.clip(2 - device, 0, 2),
    ]

    def score(j):
        s_ref = scratch[j % 2]
        q = q_ref[j * sub : (j + 1) * sub]
        q = jnp.concatenate([q, jnp.zeros((sub, 64), q.dtype)], axis=1)
        token = base + j * (sub // heads) + lax.broadcasted_iota(jnp.int32, (sub, 256), 0) // heads
        lane = lax.broadcasted_iota(jnp.int32, (sub, 256), 1)
        s0 = nt(q, near[0][:, :256])
        s0 = jnp.where(lane > jnp.maximum(token, begins[0] - 1), s0, LOW)
        s1 = nt(q, near[1][:, :256])
        s1 = jnp.where(lane >= begins[1], s1, LOW)
        s2 = nt(q, near[2][:, :256])
        s2 = jnp.where(lane[:, :128] <= token[:, :128], s2, LOW)
        s_ref[:, :256] = s0
        s_ref[:, 256:512] = s1
        s_ref[:, 512:] = s2
        top = jnp.maximum(jnp.maximum(s0, s1), jnp.concatenate([s2, s2], axis=1))
        return jnp.maximum(jnp.max(top, axis=1, keepdims=True), FLOOR)

    def mix(j, top):
        s_ref = scratch[j % 2]
        accum = jnp.zeros((sub, 256), jnp.float32)
        for part, at in enumerate((0, 256, 512)):
            wide = near[part].shape[0]
            p = jnp.exp2((s_ref[:, at : at + wide] - top) * (scale * LOG2E)).astype(jnp.bfloat16)
            v = jnp.concatenate([near[part][:, 256:], jnp.ones((wide, 128), jnp.bfloat16)], axis=1)
            accum += jnp.dot(p, v, preferred_element_type=jnp.float32)
        here = slice(j * sub, (j + 1) * sub)
        out_ref[here] = gate_ref[here, 1:2] * (accum[:, :128] / accum[:, 128:])

    tops = [score(0)]
    for j in range(blocks):
        if j + 1 < blocks:
            tops.append(score(j + 1))
        mix(j, tops[j])


def window_branch(who, q, four, two, one, paired, gates, scale, heads, block=1024, sub=256):
    total = q.shape[0]

    def row(width):
        return pl.BlockSpec((block, width), lambda i, w: (i, 0))

    def whole(array):
        return pl.BlockSpec(array.shape, lambda i, w: (0, 0))

    return pl.pallas_call(
        functools.partial(window_kernel, scale, heads),
        grid_spec=pltpu.PrefetchScalarGridSpec(
            num_scalar_prefetch=1,
            grid=(total // block,),
            in_specs=[
                row(q.shape[1]),
                whole(four),
                whole(two),
                whole(one),
                whole(paired),
                row(2),
            ],
            out_specs=row(128),
            scratch_shapes=[pltpu.VMEM((sub, 640), jnp.float32)] * 2,
        ),
        out_shape=jax.ShapeDtypeStruct((total, 128), jnp.float32),
        compiler_params=pltpu.CompilerParams(vmem_limit_bytes=GRANT),
        name="window",
        cost_estimate=pl.CostEstimate(
            flops=2 * total * 640 * 512, bytes_accessed=4000000, transcendentals=total * 640
        ),
    )(who, q, four, two, one, paired, gates)


def far_scores(heads, device, core, q, kv_ref, s_ref, base, quarters):
    block = q.shape[0]
    zeros = jnp.zeros((block, 64), q.dtype)
    queries = (
        jnp.concatenate([q, zeros], axis=1),
        jnp.concatenate([q[:, :128], zeros, q[:, 128:]], axis=1),
    )
    token = base + lax.broadcasted_iota(jnp.int32, (block, 256), 0) // heads
    lane = lax.broadcasted_iota(jnp.int32, (1, 256), 1)
    top = None
    for quarter in range(quarters):
        for g in range(kv_ref.shape[0] // 8):
            some = slice(8 * g, 8 * g + 8)
            begin = 32 * quarter
            low = kv_ref[some, begin : begin + 32].reshape(256, 128)
            begin = 128 + 32 * (quarter % 2)
            high = kv_ref[some, begin : begin + 32].reshape(256, 128)
            s = nt(queries[quarter // 2], jnp.concatenate([low, high], axis=1))
            z = 4 * quarter + (lane % 32) // 8
            owner = (2 * z + core) * 16 + 8 * g + lane // 32
            end = (owner - device) * 128 + STRIDE * (lane % 8) + STRIDE - 1
            s = jnp.where(end <= token, s, LOW)
            slot = 2 * quarter + g
            s_ref[:, 256 * slot : 256 * slot + 256] = s
            most = jnp.maximum(s[:, :128], s[:, 128:])
            top = most if top is None else jnp.maximum(top, most)
    return jnp.maximum(jnp.max(top, axis=1, keepdims=True), FLOOR)


def far_mix(scale, s_ref, top, kv_ref, quarters):
    ones = jnp.ones((256, 128), jnp.bfloat16)
    accum = jnp.zeros((s_ref.shape[0], 256), jnp.float32)
    for quarter in range(quarters):
        for g in range(kv_ref.shape[0] // 8):
            slot = 2 * quarter + g
            s = s_ref[:, 256 * slot : 256 * slot + 256]
            p = jnp.exp2((s - top) * (scale * LOG2E)).astype(jnp.bfloat16)
            begin = 192 + 32 * quarter
            v = kv_ref[8 * g : 8 * g + 8, begin : begin + 32].reshape(256, 128)
            accum += jnp.dot(
                p, jnp.concatenate([v, ones], axis=1), preferred_element_type=jnp.float32
            )
    return accum


def skewed(scale, heads, who, core, q_ref, kv_ref, scratch, finish):
    sub = scratch[0].shape[0]
    blocks = q_ref.shape[0] // sub
    plane = who[2]

    def run(quarters):
        def score(j):
            return far_scores(
                heads,
                who[0],
                core,
                q_ref[j * sub : (j + 1) * sub],
                kv_ref,
                scratch[j % 2],
                j * (sub // heads),
                quarters,
            )

        tops = [score(0)]
        for j in range(blocks):
            if j + 1 < blocks:
                tops.append(score(j + 1))
            mix = far_mix(scale, scratch[j % 2], tops[j], kv_ref, quarters)
            finish(slice(j * sub, (j + 1) * sub), mix, tops[j])

    @pl.when(plane < 4)
    def _():
        run(1)

    @pl.when((plane >= 4) & (plane < 8))
    def _():
        run(2)

    @pl.when(plane >= 8)
    def _():
        run(4)


def first_kernel(scale, heads, who, q_ref, kv_ref, acc_ref, top_ref, *scratch):
    def finish(here, accum, top):
        acc_ref[here] = accum
        top_ref[here] = jnp.broadcast_to(top, (accum.shape[0], 128))

    skewed(scale, heads, who, who[1], q_ref, kv_ref, scratch, finish)


def second_kernel(
    scale,
    heads,
    who,
    q_ref,
    kv_ref,
    acc_ref,
    top_ref,
    win_ref,
    gate_ref,
    out_hbm,
    even,
    odd,
    result,
    sems,
):
    sub = even.shape[0]

    def move(j):
        here = slice(j * sub, (j + 1) * sub)
        return pltpu.make_async_copy(result.at[here], out_hbm.at[here], sems.at[j])

    def finish(here, accum, top):
        other = top_ref[here]
        most = jnp.maximum(other, top)
        grow = jnp.exp2((other - most) * (scale * LOG2E))
        shrink = jnp.exp2((top - most) * (scale * LOG2E))
        number = acc_ref[here, :128] * grow + accum[:, :128] * shrink
        total = acc_ref[here, 128:] * grow + accum[:, 128:] * shrink
        present = total > 0.0
        compressed = jnp.where(present, number / jnp.where(present, total, 1.0), 0.0)
        result[here] = (gate_ref[here, 0:1] * compressed + win_ref[here]).astype(result.dtype)
        move(here.start // sub).start()

    skewed(scale, heads, who, 1 - who[1], q_ref, kv_ref, (even, odd), finish)
    for j in range(q_ref.shape[0] // sub):
        move(j).wait()


def first_half(who, q, kv, scale, heads, sub=256):
    total = q.shape[0]
    keys = kv.shape[0] * 128
    inside = pl.BlockSpec(memory_space=pltpu.VMEM)
    return pl.pallas_call(
        functools.partial(first_kernel, scale, heads),
        in_specs=[pl.BlockSpec(memory_space=pltpu.SMEM), inside, inside],
        out_specs=[inside, inside],
        scratch_shapes=[pltpu.VMEM((sub, keys), jnp.float32)] * 2,
        out_shape=[
            jax.ShapeDtypeStruct((total, 256), jnp.float32),
            jax.ShapeDtypeStruct((total, 128), jnp.float32),
        ],
        compiler_params=pltpu.CompilerParams(vmem_limit_bytes=GRANT),
        name="first_half",
        cost_estimate=pl.CostEstimate(
            flops=2 * total * keys * 512, bytes_accessed=3000000, transcendentals=total * keys
        ),
    )(who, q, kv)


def second_half(who, q, kv, acc, top, win, gates, scale, heads, sub=256):
    total = q.shape[0]
    keys = kv.shape[0] * 128
    inside = pl.BlockSpec(memory_space=pltpu.VMEM)
    return pl.pallas_call(
        functools.partial(second_kernel, scale, heads),
        in_specs=[pl.BlockSpec(memory_space=pltpu.SMEM)] + [inside] * 6,
        out_specs=pl.BlockSpec(memory_space=pl.ANY),
        scratch_shapes=[
            pltpu.VMEM((sub, keys), jnp.float32),
            pltpu.VMEM((sub, keys), jnp.float32),
            pltpu.VMEM((total, 128), jnp.bfloat16),
            pltpu.SemaphoreType.DMA((total // sub,)),
        ],
        out_shape=jax.ShapeDtypeStruct((total, 128), jnp.bfloat16),
        compiler_params=pltpu.CompilerParams(vmem_limit_bytes=GRANT),
        name="second_half",
        cost_estimate=pl.CostEstimate(
            flops=2 * total * keys * 512, bytes_accessed=5000000, transcendentals=total * keys
        ),
    )(who, q, kv, acc, top, win, gates)


def local(
    queries, keys, values, key_first, key_second, value_first, value_second, gate_table, gate_index
):
    rows, heads, depth = queries.shape
    outer, inner = lax.axis_index("sa"), lax.axis_index("sb")
    core = outer % 2
    device = outer * lax.axis_size("sb") + inner
    who = jnp.stack([device, core, outer // 2]).astype(jnp.int32)
    planes = lax.axis_size("sa") // 2
    scale = depth ** (-0.5)
    paired = pair(keys, values)
    one = shifted(paired, ("sa", "sb"), 1)
    kfirst = key_first.T
    hidden = own_blocks(paired, kfirst, value_first)
    payload = summary(one, hidden, kfirst, key_second, value_first, value_second, planes)
    payload, later, again = lax.optimization_barrier((payload, one, paired))
    groups = [[2 * z + c for z in range(planes)] for c in range(2)]
    column = lax.all_to_all(payload, "sa", 0, 0, axis_index_groups=groups)
    four = shifted(again, ("sa", "sb"), 4)
    two = shifted(jnp.concatenate([later, again], axis=0), ("sa", "sb"), 2)
    query_rows = queries.reshape(rows * heads, depth)
    chosen = gate_index.reshape(rows * heads)
    onehot = (chosen[:, None] == lax.iota(jnp.int32, gate_table.shape[0])[None, :]).astype(
        jnp.float32
    )
    gates = jnp.sum(onehot[:, :, None] * gate_table[None, :, :], axis=1)
    copies = pack(column, lax.axis_size("sb"))
    mine = lax.all_to_all(copies, "sb", 0, 0)
    win = window_branch(who, query_rows, four, two, later, again, gates, scale, heads)
    mine, win = lax.optimization_barrier((mine, win))
    other = lax.ppermute(mine, "sa", [(i, i ^ 1) for i in range(2 * planes)])
    acc, top = first_half(who, query_rows, mine, scale, heads)
    mixed = second_half(who, query_rows, other, acc, top, win, gates, scale, heads)
    return mixed.reshape(rows, heads, values.shape[1])


def solution(mesh):
    in_specs = (
        P(("sa", "sb"), None, None),
        P(("sa", "sb"), None),
        P(("sa", "sb"), None),
        P(),
        P(),
        P(),
        P(),
        P(),
        P(("sa", "sb"), None),
    )
    out_specs = P(("sa", "sb"), None, None)
    return jax.shard_map(local, mesh=mesh, in_specs=in_specs, out_specs=out_specs, check_vma=False)
```

```python
import functools

import jax
import jax.numpy as jnp
from jax import lax
from jax.experimental import pallas as pl
from jax.experimental.pallas import tpu as pltpu
from jax.sharding import PartitionSpec as P


STRIDE = 16
LOG2E = 1.4426950408889634
LOW = -1e30
FLOOR = -1e29
GRANT = 20 << 20


def nt(a, b):
    return lax.dot_general(a, b, (((1,), (1,)), ((), ())), preferred_element_type=jnp.float32)


def shifted(shard, axis, by):
    size = lax.axis_size(axis)
    pairs = [(i, i + by) for i in range(size) if 0 <= i + by < size]
    return lax.ppermute(shard, axis, pairs)


def pair_kernel(keys_hbm, values_hbm, out_ref, keys, sems):
    loads = [
        pltpu.make_async_copy(keys_hbm, keys, sems.at[0]),
        pltpu.make_async_copy(values_hbm, out_ref.at[:, 256:], sems.at[1]),
    ]
    for load in loads:
        load.start()
    out_ref[:, 192:256] = jnp.zeros((out_ref.shape[0], 64), out_ref.dtype)
    loads[0].wait()
    out_ref[:, :192] = keys[...].astype(jnp.float32).T.astype(out_ref.dtype)
    loads[1].wait()


def pair(keys, values):
    return pl.pallas_call(
        pair_kernel,
        in_specs=[pl.BlockSpec(memory_space=pltpu.HBM)] * 2,
        out_specs=pl.BlockSpec(memory_space=pltpu.VMEM),
        out_shape=jax.ShapeDtypeStruct((values.shape[0], 384), keys.dtype),
        scratch_shapes=[
            pltpu.VMEM(keys.shape, keys.dtype),
            pltpu.SemaphoreType.DMA((2,)),
        ],
        compiler_params=pltpu.CompilerParams(vmem_limit_bytes=GRANT),
        name="pair",
    )(keys, values)


def silu(x):
    return x * (1.0 / (1.0 + jnp.exp(-x)))


def segments(wide_ref, count):
    keys, values = [], []
    for first in range(STRIDE):
        some = [wide_ref[part, pl.ds(first, count, stride=STRIDE), :] for part in range(3)]
        keys.append(jnp.concatenate([some[0], some[1][:, :64]], axis=1))
        values.append(some[2])
    keys = jnp.concatenate(keys, axis=1).astype(jnp.bfloat16)
    values = jnp.concatenate(values, axis=1).astype(jnp.bfloat16)
    return keys, values


def own_kernel(
    pair_ref, kfirst_ref, vfirst_hbm, hidden_ref, kfront_ref, vfront_ref, wide, vback_ref, sems
):
    tall = vback_ref.shape[0]
    loads = [
        pltpu.make_async_copy(vfirst_hbm.at[tall:], vback_ref, sems.at[0]),
        pltpu.make_async_copy(vfirst_hbm.at[:tall], vfront_ref, sems.at[1]),
    ]
    for load in loads:
        load.start()
    half_keys = kfirst_ref.shape[1] // 2
    count = pair_ref.shape[0] // STRIDE
    for part in range(3):
        lanes = slice(128 * part, 128 * part + 128)
        wide[part] = pair_ref[:, lanes].astype(jnp.float32)
    keys, values = segments(wide, count)
    nothing = jnp.zeros((count, 64), jnp.float32)
    back = nt(keys, kfirst_ref[:, half_keys:])
    ahead = nt(keys, kfirst_ref[:, :half_keys])
    kfront_ref[...] = kfirst_ref[:, :half_keys]
    loads[0].wait()
    value = jnp.dot(values, vback_ref[...], preferred_element_type=jnp.float32)
    back = jnp.concatenate([back, nothing, value], axis=1)
    loads[1].wait()
    value = jnp.dot(values, vfront_ref[...], preferred_element_type=jnp.float32)
    ahead = jnp.concatenate([ahead, nothing, value], axis=1)
    row = lax.broadcasted_iota(jnp.int32, back.shape, 0)
    hidden_ref[...] = back + jnp.where(row == 0, 0.0, pltpu.roll(ahead, 1, 0))


def own_blocks(paired, kfirst, vfirst):
    rows = paired.shape[0]
    inside = pl.BlockSpec(memory_space=pltpu.VMEM)
    return pl.pallas_call(
        own_kernel,
        in_specs=[inside, inside, pl.BlockSpec(memory_space=pltpu.HBM)],
        out_specs=[inside] * 3,
        out_shape=[
            jax.ShapeDtypeStruct((rows // STRIDE, 384), jnp.float32),
            jax.ShapeDtypeStruct((kfirst.shape[0], kfirst.shape[1] // 2), kfirst.dtype),
            jax.ShapeDtypeStruct((vfirst.shape[0] // 2, vfirst.shape[1]), vfirst.dtype),
        ],
        scratch_shapes=[
            pltpu.VMEM((3, rows, 128), jnp.float32),
            pltpu.VMEM((vfirst.shape[0] // 2, vfirst.shape[1]), vfirst.dtype),
            pltpu.SemaphoreType.DMA((2,)),
        ],
        compiler_params=pltpu.CompilerParams(vmem_limit_bytes=GRANT),
        name="own_blocks",
        cost_estimate=pl.CostEstimate(
            flops=1000000000, bytes_accessed=8000000, transcendentals=0
        ),
    )(paired, kfirst, vfirst)


def summary_kernel(
    before_ref,
    hidden_ref,
    kfront_ref,
    ksecond_hbm,
    vfront_ref,
    vsecond_hbm,
    out_ref,
    wide,
    ksecond,
    vsecond,
    sems,
):
    loads = [
        pltpu.make_async_copy(ksecond_hbm, ksecond, sems.at[0]),
        pltpu.make_async_copy(vsecond_hbm, vsecond, sems.at[1]),
    ]
    for load in loads:
        load.start()
    rows = before_ref.shape[0]
    count = hidden_ref.shape[0]
    for part in range(3):
        lanes = slice(128 * part, 128 * part + 128)
        wide[part] = before_ref[:, lanes].astype(jnp.float32)
    keys, values = segments(wide, rows // STRIDE)
    ahead = nt(keys, kfront_ref[...])
    value = jnp.dot(values, vfront_ref[...], preferred_element_type=jnp.float32)
    ahead = jnp.concatenate([ahead, jnp.zeros((count, 64), jnp.float32), value], axis=1)
    row = lax.broadcasted_iota(jnp.int32, ahead.shape, 0)
    hidden = hidden_ref[...] + jnp.where(row == 0, pltpu.roll(ahead, 1, 0), 0.0)
    hidden = silu(hidden).astype(jnp.bfloat16)
    for load in loads:
        load.wait()
    key = jnp.dot(hidden[:, :192], ksecond[...], preferred_element_type=jnp.float32)
    value = jnp.dot(hidden[:, 256:], vsecond[...], preferred_element_type=jnp.float32)
    high = jnp.concatenate([key[:, 128:], jnp.zeros((count, 64), jnp.float32)], axis=1)
    payload = jnp.concatenate([key[:, :128], high, value], axis=0).astype(out_ref.dtype)
    for copy in range(out_ref.shape[0]):
        out_ref[copy] = payload


def summary(before, hidden, kfront, key_second, vfront, value_second, copies):
    inside = pl.BlockSpec(memory_space=pltpu.VMEM)
    outside = pl.BlockSpec(memory_space=pltpu.HBM)
    return pl.pallas_call(
        summary_kernel,
        in_specs=[inside, inside, inside, outside, inside, outside],
        out_specs=inside,
        out_shape=jax.ShapeDtypeStruct((copies, 3 * hidden.shape[0], 128), jnp.bfloat16),
        scratch_shapes=[
            pltpu.VMEM((3,) + (before.shape[0], 128), jnp.float32),
            pltpu.VMEM(key_second.shape, jnp.bfloat16),
            pltpu.VMEM(value_second.shape, jnp.bfloat16),
            pltpu.SemaphoreType.DMA((2,)),
        ],
        compiler_params=pltpu.CompilerParams(vmem_limit_bytes=GRANT),
        name="summary",
    )(before, hidden, kfront, key_second, vfront, value_second)


def pack_kernel(column_ref, out_hbm, packed, sems):
    planes = column_ref.shape[0]
    half = planes // 2
    count = column_ref.shape[1] // 3
    low = column_ref[:, :count].astype(jnp.float32).reshape(planes * count, 128)
    high = column_ref[:, count : 2 * count].astype(jnp.float32)
    high = jnp.concatenate(
        [
            high[:half].reshape(half * count, 128)[:, :64],
            high[half:].reshape(half * count, 128)[:, :64],
        ],
        axis=1,
    )
    value = column_ref[:, 2 * count :].astype(jnp.float32).reshape(planes * count, 128)
    packed[...] = jnp.concatenate([low, high, value], axis=0).astype(packed.dtype)
    moves = [
        pltpu.make_async_copy(packed, out_hbm.at[copy], sems.at[copy])
        for copy in range(out_hbm.shape[0])
    ]
    for move in moves:
        move.start()
    for move in moves:
        move.wait()


def pack(column, copies):
    planes, rows, lanes = column.shape
    size = planes * rows * 5 // 6
    return pl.pallas_call(
        pack_kernel,
        in_specs=[pl.BlockSpec(memory_space=pltpu.VMEM)],
        out_specs=pl.BlockSpec(memory_space=pl.ANY),
        out_shape=jax.ShapeDtypeStruct((copies, size, lanes), column.dtype),
        scratch_shapes=[
            pltpu.VMEM((size, lanes), column.dtype),
            pltpu.SemaphoreType.DMA((copies,)),
        ],
        compiler_params=pltpu.CompilerParams(vmem_limit_bytes=GRANT),
        name="pack",
    )(column)


def window_kernel(
    scale, heads, who, q_ref, four_ref, two_ref, one_ref, pair_ref, gate_ref, out_ref, *scratch
):
    sub = scratch[0].shape[0]
    size = pair_ref.shape[0]
    blocks = q_ref.shape[0] // sub
    device = who[0]
    base = pl.program_id(0) * (q_ref.shape[0] // heads)
    near = (
        jnp.concatenate([four_ref[...], two_ref[:size]], axis=0),
        jnp.concatenate([two_ref[size:], one_ref[...]], axis=0),
        pair_ref[...],
    )
    begins = [
        size * jnp.clip(4 - device, 0, 2),
        size * jnp.clip(2 - device, 0, 2),
    ]

    def score(j):
        s_ref = scratch[j % 2]
        q = q_ref[j * sub : (j + 1) * sub]
        q = jnp.concatenate([q, jnp.zeros((sub, 64), q.dtype)], axis=1)
        token = base + j * (sub // heads) + lax.broadcasted_iota(jnp.int32, (sub, 256), 0) // heads
        lane = lax.broadcasted_iota(jnp.int32, (sub, 256), 1)
        s0 = nt(q, near[0][:, :256])
        s0 = jnp.where(lane > jnp.maximum(token, begins[0] - 1), s0, LOW)
        s1 = nt(q, near[1][:, :256])
        s1 = jnp.where(lane >= begins[1], s1, LOW)
        s2 = nt(q, near[2][:, :256])
        s2 = jnp.where(lane[:, :128] <= token[:, :128], s2, LOW)
        s_ref[:, :256] = s0
        s_ref[:, 256:512] = s1
        s_ref[:, 512:] = s2
        top = jnp.maximum(jnp.maximum(s0, s1), jnp.concatenate([s2, s2], axis=1))
        return jnp.maximum(jnp.max(top, axis=1, keepdims=True), FLOOR)

    def mix(j, top):
        s_ref = scratch[j % 2]
        accum = jnp.zeros((sub, 256), jnp.float32)
        for part, at in enumerate((0, 256, 512)):
            wide = near[part].shape[0]
            p = jnp.exp2((s_ref[:, at : at + wide] - top) * (scale * LOG2E)).astype(jnp.bfloat16)
            v = jnp.concatenate([near[part][:, 256:], jnp.ones((wide, 128), jnp.bfloat16)], axis=1)
            accum += jnp.dot(p, v, preferred_element_type=jnp.float32)
        here = slice(j * sub, (j + 1) * sub)
        out_ref[here] = gate_ref[here, 1:2] * (accum[:, :128] / accum[:, 128:])

    tops = [score(0)]
    for j in range(blocks):
        if j + 1 < blocks:
            tops.append(score(j + 1))
        mix(j, tops[j])


def window_branch(who, q, four, two, one, paired, gates, scale, heads, block=1024, sub=256):
    total = q.shape[0]

    def row(width):
        return pl.BlockSpec((block, width), lambda i, w: (i, 0))

    def whole(array):
        return pl.BlockSpec(array.shape, lambda i, w: (0, 0))

    return pl.pallas_call(
        functools.partial(window_kernel, scale, heads),
        grid_spec=pltpu.PrefetchScalarGridSpec(
            num_scalar_prefetch=1,
            grid=(total // block,),
            in_specs=[
                row(q.shape[1]),
                whole(four),
                whole(two),
                whole(one),
                whole(paired),
                row(2),
            ],
            out_specs=row(128),
            scratch_shapes=[pltpu.VMEM((sub, 640), jnp.float32)] * 2,
        ),
        out_shape=jax.ShapeDtypeStruct((total, 128), jnp.float32),
        compiler_params=pltpu.CompilerParams(vmem_limit_bytes=GRANT),
        name="window",
        cost_estimate=pl.CostEstimate(
            flops=2 * total * 640 * 512, bytes_accessed=4000000, transcendentals=total * 640
        ),
    )(who, q, four, two, one, paired, gates)


def far_scores(heads, device, core, q, kv_ref, s_ref, base, quarters):
    block = q.shape[0]
    zeros = jnp.zeros((block, 64), q.dtype)
    queries = (
        jnp.concatenate([q, zeros], axis=1),
        jnp.concatenate([q[:, :128], zeros, q[:, 128:]], axis=1),
    )
    token = base + lax.broadcasted_iota(jnp.int32, (block, 256), 0) // heads
    lane = lax.broadcasted_iota(jnp.int32, (1, 256), 1)
    top = None
    for quarter in range(quarters):
        for g in range(kv_ref.shape[0] // 8):
            some = slice(8 * g, 8 * g + 8)
            begin = 32 * quarter
            low = kv_ref[some, begin : begin + 32].reshape(256, 128)
            begin = 128 + 32 * (quarter % 2)
            high = kv_ref[some, begin : begin + 32].reshape(256, 128)
            s = nt(queries[quarter // 2], jnp.concatenate([low, high], axis=1))
            z = 4 * quarter + (lane % 32) // 8
            owner = (2 * z + core) * 16 + 8 * g + lane // 32
            end = (owner - device) * 128 + STRIDE * (lane % 8) + STRIDE - 1
            s = jnp.where(end <= token, s, LOW)
            slot = 2 * quarter + g
            s_ref[:, 256 * slot : 256 * slot + 256] = s
            most = jnp.maximum(s[:, :128], s[:, 128:])
            top = most if top is None else jnp.maximum(top, most)
    return jnp.maximum(jnp.max(top, axis=1, keepdims=True), FLOOR)


def far_mix(scale, s_ref, top, kv_ref, quarters):
    ones = jnp.ones((256, 128), jnp.bfloat16)
    accum = jnp.zeros((s_ref.shape[0], 256), jnp.float32)
    for quarter in range(quarters):
        for g in range(kv_ref.shape[0] // 8):
            slot = 2 * quarter + g
            s = s_ref[:, 256 * slot : 256 * slot + 256]
            p = jnp.exp2((s - top) * (scale * LOG2E)).astype(jnp.bfloat16)
            begin = 192 + 32 * quarter
            v = kv_ref[8 * g : 8 * g + 8, begin : begin + 32].reshape(256, 128)
            accum += jnp.dot(
                p, jnp.concatenate([v, ones], axis=1), preferred_element_type=jnp.float32
            )
    return accum


def skewed(scale, heads, who, core, q_ref, kv_ref, scratch, finish):
    sub = scratch[0].shape[0]
    blocks = q_ref.shape[0] // sub
    plane = who[2]

    def run(quarters):
        def score(j):
            return far_scores(
                heads,
                who[0],
                core,
                q_ref[j * sub : (j + 1) * sub],
                kv_ref,
                scratch[j % 2],
                j * (sub // heads),
                quarters,
            )

        tops = [score(0)]
        for j in range(blocks):
            if j + 1 < blocks:
                tops.append(score(j + 1))
            mix = far_mix(scale, scratch[j % 2], tops[j], kv_ref, quarters)
            finish(slice(j * sub, (j + 1) * sub), mix, tops[j])

    @pl.when(plane < 4)
    def _():
        run(1)

    @pl.when((plane >= 4) & (plane < 8))
    def _():
        run(2)

    @pl.when(plane >= 8)
    def _():
        run(4)


def first_kernel(scale, heads, who, q_ref, kv_ref, acc_ref, top_ref, *scratch):
    def finish(here, accum, top):
        acc_ref[here] = accum
        top_ref[here] = jnp.broadcast_to(top, (accum.shape[0], 128))

    skewed(scale, heads, who, who[1], q_ref, kv_ref, scratch, finish)


def second_kernel(
    scale,
    heads,
    who,
    q_ref,
    kv_ref,
    acc_ref,
    top_ref,
    win_ref,
    gate_ref,
    out_hbm,
    even,
    odd,
    result,
    sems,
):
    sub = even.shape[0]

    def move(j):
        here = slice(j * sub, (j + 1) * sub)
        return pltpu.make_async_copy(result.at[here], out_hbm.at[here], sems.at[j])

    def finish(here, accum, top):
        other = top_ref[here]
        most = jnp.maximum(other, top)
        grow = jnp.exp2((other - most) * (scale * LOG2E))
        shrink = jnp.exp2((top - most) * (scale * LOG2E))
        number = acc_ref[here, :128] * grow + accum[:, :128] * shrink
        total = acc_ref[here, 128:] * grow + accum[:, 128:] * shrink
        present = total > 0.0
        compressed = jnp.where(present, number / jnp.where(present, total, 1.0), 0.0)
        result[here] = (gate_ref[here, 0:1] * compressed + win_ref[here]).astype(result.dtype)
        move(here.start // sub).start()

    skewed(scale, heads, who, 1 - who[1], q_ref, kv_ref, (even, odd), finish)
    for j in range(q_ref.shape[0] // sub):
        move(j).wait()


def first_half(who, q, kv, scale, heads, sub=256):
    total = q.shape[0]
    keys = kv.shape[0] * 128
    inside = pl.BlockSpec(memory_space=pltpu.VMEM)
    return pl.pallas_call(
        functools.partial(first_kernel, scale, heads),
        in_specs=[pl.BlockSpec(memory_space=pltpu.SMEM), inside, inside],
        out_specs=[inside, inside],
        scratch_shapes=[pltpu.VMEM((sub, keys), jnp.float32)] * 2,
        out_shape=[
            jax.ShapeDtypeStruct((total, 256), jnp.float32),
            jax.ShapeDtypeStruct((total, 128), jnp.float32),
        ],
        compiler_params=pltpu.CompilerParams(vmem_limit_bytes=GRANT),
        name="first_half",
        cost_estimate=pl.CostEstimate(
            flops=2 * total * keys * 512, bytes_accessed=3000000, transcendentals=total * keys
        ),
    )(who, q, kv)


def second_half(who, q, kv, acc, top, win, gates, scale, heads, sub=256):
    total = q.shape[0]
    keys = kv.shape[0] * 128
    inside = pl.BlockSpec(memory_space=pltpu.VMEM)
    return pl.pallas_call(
        functools.partial(second_kernel, scale, heads),
        in_specs=[pl.BlockSpec(memory_space=pltpu.SMEM)] + [inside] * 6,
        out_specs=pl.BlockSpec(memory_space=pl.ANY),
        scratch_shapes=[
            pltpu.VMEM((sub, keys), jnp.float32),
            pltpu.VMEM((sub, keys), jnp.float32),
            pltpu.VMEM((total, 128), jnp.bfloat16),
            pltpu.SemaphoreType.DMA((total // sub,)),
        ],
        out_shape=jax.ShapeDtypeStruct((total, 128), jnp.bfloat16),
        compiler_params=pltpu.CompilerParams(vmem_limit_bytes=GRANT),
        name="second_half",
        cost_estimate=pl.CostEstimate(
            flops=2 * total * keys * 512, bytes_accessed=5000000, transcendentals=total * keys
        ),
    )(who, q, kv, acc, top, win, gates)


def local(
    queries, keys, values, key_first, key_second, value_first, value_second, gate_table, gate_index
):
    rows, heads, depth = queries.shape
    outer, inner = lax.axis_index("sa"), lax.axis_index("sb")
    core = outer % 2
    device = outer * lax.axis_size("sb") + inner
    who = jnp.stack([device, core, outer // 2]).astype(jnp.int32)
    planes = lax.axis_size("sa") // 2
    scale = depth ** (-0.5)

    def stay(x):
        return pltpu.with_memory_space_constraint(x, pltpu.HBM)

    paired = pair(stay(keys.T), stay(values))
    one = shifted(paired, ("sa", "sb"), 1)
    kfirst = key_first.T
    hidden, kfront, vfront = own_blocks(paired, kfirst, stay(value_first))
    payload = summary(
        one, hidden, kfront, stay(key_second), vfront, stay(value_second), planes
    )
    payload, later, again = lax.optimization_barrier((payload, one, paired))
    groups = [[2 * z + c for z in range(planes)] for c in range(2)]
    column = lax.all_to_all(payload, "sa", 0, 0, axis_index_groups=groups)
    four = shifted(again, ("sa", "sb"), 4)
    two = shifted(jnp.concatenate([later, again], axis=0), ("sa", "sb"), 2)
    query_rows = queries.reshape(rows * heads, depth)
    chosen = gate_index.reshape(rows * heads)
    onehot = (chosen[:, None] == lax.iota(jnp.int32, gate_table.shape[0])[None, :]).astype(
        jnp.float32
    )
    gates = jnp.sum(onehot[:, :, None] * gate_table[None, :, :], axis=1)
    copies = pack(column, lax.axis_size("sb"))
    mine = lax.all_to_all(copies, "sb", 0, 0)
    win = window_branch(who, query_rows, four, two, later, again, gates, scale, heads)
    mine, win = lax.optimization_barrier((mine, win))
    other = lax.ppermute(mine, "sa", [(i, i ^ 1) for i in range(2 * planes)])
    acc, top = first_half(who, query_rows, mine, scale, heads)
    mixed = second_half(who, query_rows, other, acc, top, win, gates, scale, heads)
    return mixed.reshape(rows, heads, values.shape[1])


def solution(mesh):
    in_specs = (
        P(("sa", "sb"), None, None),
        P(("sa", "sb"), None),
        P(("sa", "sb"), None),
        P(),
        P(),
        P(),
        P(),
        P(),
        P(("sa", "sb"), None),
    )
    out_specs = P(("sa", "sb"), None, None)
    return jax.shard_map(local, mesh=mesh, in_specs=in_specs, out_specs=out_specs, check_vma=False)
```

```python
import functools

import jax
import jax.numpy as jnp
from jax import lax
from jax.experimental import pallas as pl
from jax.experimental.pallas import tpu as pltpu
from jax.sharding import PartitionSpec as P


STRIDE = 16
LOG2E = 1.4426950408889634
LOW = -1e30
FLOOR = -1e29
GRANT = 20 << 20


def nt(a, b):
    return lax.dot_general(a, b, (((1,), (1,)), ((), ())), preferred_element_type=jnp.float32)


def shifted(shard, axis, by):
    size = lax.axis_size(axis)
    pairs = [(i, i + by) for i in range(size) if 0 <= i + by < size]
    return lax.ppermute(shard, axis, pairs)


def pair_kernel(keys_hbm, values_hbm, out_ref, keys, sems):
    loads = [
        pltpu.make_async_copy(keys_hbm, keys, sems.at[0]),
        pltpu.make_async_copy(values_hbm, out_ref.at[:, 256:], sems.at[1]),
    ]
    for load in loads:
        load.start()
    out_ref[:, 192:256] = jnp.zeros((out_ref.shape[0], 64), out_ref.dtype)
    loads[0].wait()
    out_ref[:, :192] = keys[...].astype(jnp.float32).T.astype(out_ref.dtype)
    loads[1].wait()


def pair(keys, values):
    return pl.pallas_call(
        pair_kernel,
        in_specs=[pl.BlockSpec(memory_space=pltpu.HBM)] * 2,
        out_specs=pl.BlockSpec(memory_space=pltpu.VMEM),
        out_shape=jax.ShapeDtypeStruct((values.shape[0], 384), keys.dtype),
        scratch_shapes=[
            pltpu.VMEM(keys.shape, keys.dtype),
            pltpu.SemaphoreType.DMA((2,)),
        ],
        compiler_params=pltpu.CompilerParams(vmem_limit_bytes=GRANT),
        name="pair",
    )(keys, values)


def silu(x):
    return x * (1.0 / (1.0 + jnp.exp(-x)))


def segments(wide_ref, count):
    keys, values = [], []
    for first in range(STRIDE):
        some = [wide_ref[part, pl.ds(first, count, stride=STRIDE), :] for part in range(3)]
        keys.append(jnp.concatenate([some[0], some[1][:, :64]], axis=1))
        values.append(some[2])
    keys = jnp.concatenate(keys, axis=1).astype(jnp.bfloat16)
    values = jnp.concatenate(values, axis=1).astype(jnp.bfloat16)
    return keys, values


def own_kernel(
    pair_ref, kfirst_ref, vfirst_hbm, hidden_ref, kfront_ref, vfront_ref, wide, vback_ref, sems
):
    tall = vback_ref.shape[0]
    loads = [
        pltpu.make_async_copy(vfirst_hbm.at[tall:], vback_ref, sems.at[0]),
        pltpu.make_async_copy(vfirst_hbm.at[:tall], vfront_ref, sems.at[1]),
    ]
    for load in loads:
        load.start()
    half_keys = kfirst_ref.shape[1] // 2
    count = pair_ref.shape[0] // STRIDE
    for part in range(3):
        lanes = slice(128 * part, 128 * part + 128)
        wide[part] = pair_ref[:, lanes].astype(jnp.float32)
    keys, values = segments(wide, count)
    nothing = jnp.zeros((count, 64), jnp.float32)
    back = nt(keys, kfirst_ref[:, half_keys:])
    ahead = nt(keys, kfirst_ref[:, :half_keys])
    kfront_ref[...] = kfirst_ref[:, :half_keys]
    loads[0].wait()
    value = jnp.dot(values, vback_ref[...], preferred_element_type=jnp.float32)
    back = jnp.concatenate([back, nothing, value], axis=1)
    loads[1].wait()
    value = jnp.dot(values, vfront_ref[...], preferred_element_type=jnp.float32)
    ahead = jnp.concatenate([ahead, nothing, value], axis=1)
    row = lax.broadcasted_iota(jnp.int32, back.shape, 0)
    hidden_ref[...] = back + jnp.where(row == 0, 0.0, pltpu.roll(ahead, 1, 0))


def own_blocks(paired, kfirst, vfirst):
    rows = paired.shape[0]
    inside = pl.BlockSpec(memory_space=pltpu.VMEM)
    return pl.pallas_call(
        own_kernel,
        in_specs=[inside, inside, pl.BlockSpec(memory_space=pltpu.HBM)],
        out_specs=[inside] * 3,
        out_shape=[
            jax.ShapeDtypeStruct((rows // STRIDE, 384), jnp.float32),
            jax.ShapeDtypeStruct((kfirst.shape[0], kfirst.shape[1] // 2), kfirst.dtype),
            jax.ShapeDtypeStruct((vfirst.shape[0] // 2, vfirst.shape[1]), vfirst.dtype),
        ],
        scratch_shapes=[
            pltpu.VMEM((3, rows, 128), jnp.float32),
            pltpu.VMEM((vfirst.shape[0] // 2, vfirst.shape[1]), vfirst.dtype),
            pltpu.SemaphoreType.DMA((2,)),
        ],
        compiler_params=pltpu.CompilerParams(vmem_limit_bytes=GRANT),
        name="own_blocks",
        cost_estimate=pl.CostEstimate(
            flops=1000000000, bytes_accessed=8000000, transcendentals=0
        ),
    )(paired, kfirst, vfirst)


def summary_kernel(
    before_ref,
    hidden_ref,
    kfront_ref,
    ksecond_hbm,
    vfront_ref,
    vsecond_hbm,
    out_ref,
    wide,
    ksecond,
    vsecond,
    sems,
):
    loads = [
        pltpu.make_async_copy(ksecond_hbm, ksecond, sems.at[0]),
        pltpu.make_async_copy(vsecond_hbm, vsecond, sems.at[1]),
    ]
    for load in loads:
        load.start()
    rows = before_ref.shape[0]
    count = hidden_ref.shape[0]
    for part in range(3):
        lanes = slice(128 * part, 128 * part + 128)
        wide[part] = before_ref[:, lanes].astype(jnp.float32)
    keys, values = segments(wide, rows // STRIDE)
    ahead = nt(keys, kfront_ref[...])
    value = jnp.dot(values, vfront_ref[...], preferred_element_type=jnp.float32)
    ahead = jnp.concatenate([ahead, jnp.zeros((count, 64), jnp.float32), value], axis=1)
    row = lax.broadcasted_iota(jnp.int32, ahead.shape, 0)
    hidden = hidden_ref[...] + jnp.where(row == 0, pltpu.roll(ahead, 1, 0), 0.0)
    hidden = silu(hidden).astype(jnp.bfloat16)
    for load in loads:
        load.wait()
    key = jnp.dot(hidden[:, :192], ksecond[...], preferred_element_type=jnp.float32)
    value = jnp.dot(hidden[:, 256:], vsecond[...], preferred_element_type=jnp.float32)
    high = jnp.concatenate([key[:, 128:], jnp.zeros((count, 64), jnp.float32)], axis=1)
    payload = jnp.concatenate([key[:, :128], high, value], axis=0).astype(out_ref.dtype)
    for copy in range(out_ref.shape[0]):
        out_ref[copy] = payload


def summary(before, hidden, kfront, key_second, vfront, value_second, copies):
    inside = pl.BlockSpec(memory_space=pltpu.VMEM)
    outside = pl.BlockSpec(memory_space=pltpu.HBM)
    return pl.pallas_call(
        summary_kernel,
        in_specs=[inside, inside, inside, outside, inside, outside],
        out_specs=inside,
        out_shape=jax.ShapeDtypeStruct((copies, 3 * hidden.shape[0], 128), jnp.bfloat16),
        scratch_shapes=[
            pltpu.VMEM((3,) + (before.shape[0], 128), jnp.float32),
            pltpu.VMEM(key_second.shape, jnp.bfloat16),
            pltpu.VMEM(value_second.shape, jnp.bfloat16),
            pltpu.SemaphoreType.DMA((2,)),
        ],
        compiler_params=pltpu.CompilerParams(vmem_limit_bytes=GRANT),
        name="summary",
    )(before, hidden, kfront, key_second, vfront, value_second)


def pack_kernel(column_ref, out_hbm, packed, sems):
    planes = column_ref.shape[0]
    half = planes // 2
    count = column_ref.shape[1] // 3
    low = column_ref[:, :count].astype(jnp.float32).reshape(planes * count, 128)
    high = column_ref[:, count : 2 * count].astype(jnp.float32)
    high = jnp.concatenate(
        [
            high[:half].reshape(half * count, 128)[:, :64],
            high[half:].reshape(half * count, 128)[:, :64],
        ],
        axis=1,
    )
    value = column_ref[:, 2 * count :].astype(jnp.float32).reshape(planes * count, 128)
    packed[...] = jnp.concatenate([low, high, value], axis=0).astype(packed.dtype)
    moves = [
        pltpu.make_async_copy(packed, out_hbm.at[copy], sems.at[copy])
        for copy in range(out_hbm.shape[0])
    ]
    for move in moves:
        move.start()
    for move in moves:
        move.wait()


def pack(column, copies):
    planes, rows, lanes = column.shape
    size = planes * rows * 5 // 6
    return pl.pallas_call(
        pack_kernel,
        in_specs=[pl.BlockSpec(memory_space=pltpu.VMEM)],
        out_specs=pl.BlockSpec(memory_space=pl.ANY),
        out_shape=jax.ShapeDtypeStruct((copies, size, lanes), column.dtype),
        scratch_shapes=[
            pltpu.VMEM((size, lanes), column.dtype),
            pltpu.SemaphoreType.DMA((copies,)),
        ],
        compiler_params=pltpu.CompilerParams(vmem_limit_bytes=GRANT),
        name="pack",
    )(column)


def window_kernel(
    scale, heads, who, q_ref, four_ref, two_ref, one_ref, pair_ref, gate_ref, out_ref, *scratch
):
    sub = scratch[0].shape[0]
    size = pair_ref.shape[0]
    blocks = q_ref.shape[0] // sub
    device = who[0]
    base = pl.program_id(0) * (q_ref.shape[0] // heads)
    near = (
        jnp.concatenate([four_ref[...], two_ref[:size]], axis=0),
        jnp.concatenate([two_ref[size:], one_ref[...]], axis=0),
        pair_ref[...],
    )
    begins = [
        size * jnp.clip(4 - device, 0, 2),
        size * jnp.clip(2 - device, 0, 2),
    ]

    def score(j):
        s_ref = scratch[j % 2]
        q = q_ref[j * sub : (j + 1) * sub]
        q = jnp.concatenate([q, jnp.zeros((sub, 64), q.dtype)], axis=1)
        token = base + j * (sub // heads) + lax.broadcasted_iota(jnp.int32, (sub, 256), 0) // heads
        lane = lax.broadcasted_iota(jnp.int32, (sub, 256), 1)
        s0 = nt(q, near[0][:, :256])
        s0 = jnp.where(lane > jnp.maximum(token, begins[0] - 1), s0, LOW)
        s1 = nt(q, near[1][:, :256])
        s1 = jnp.where(lane >= begins[1], s1, LOW)
        s2 = nt(q, near[2][:, :256])
        s2 = jnp.where(lane[:, :128] <= token[:, :128], s2, LOW)
        s_ref[:, :256] = s0
        s_ref[:, 256:512] = s1
        s_ref[:, 512:] = s2
        top = jnp.maximum(jnp.maximum(s0, s1), jnp.concatenate([s2, s2], axis=1))
        return jnp.maximum(jnp.max(top, axis=1, keepdims=True), FLOOR)

    def mix(j, top):
        s_ref = scratch[j % 2]
        accum = jnp.zeros((sub, 256), jnp.float32)
        for part, at in enumerate((0, 256, 512)):
            wide = near[part].shape[0]
            p = jnp.exp2((s_ref[:, at : at + wide] - top) * (scale * LOG2E)).astype(jnp.bfloat16)
            v = jnp.concatenate([near[part][:, 256:], jnp.ones((wide, 128), jnp.bfloat16)], axis=1)
            accum += jnp.dot(p, v, preferred_element_type=jnp.float32)
        here = slice(j * sub, (j + 1) * sub)
        out_ref[here] = gate_ref[here, 1:2] * (accum[:, :128] / accum[:, 128:])

    tops = [score(0)]
    for j in range(blocks):
        if j + 1 < blocks:
            tops.append(score(j + 1))
        mix(j, tops[j])


def window_branch(who, q, four, two, one, paired, gates, scale, heads, block=1024, sub=256):
    total = q.shape[0]

    def row(width):
        return pl.BlockSpec((block, width), lambda i, w: (i, 0))

    def whole(array):
        return pl.BlockSpec(array.shape, lambda i, w: (0, 0))

    return pl.pallas_call(
        functools.partial(window_kernel, scale, heads),
        grid_spec=pltpu.PrefetchScalarGridSpec(
            num_scalar_prefetch=1,
            grid=(total // block,),
            in_specs=[
                row(q.shape[1]),
                whole(four),
                whole(two),
                whole(one),
                whole(paired),
                row(2),
            ],
            out_specs=row(128),
            scratch_shapes=[pltpu.VMEM((sub, 640), jnp.float32)] * 2,
        ),
        out_shape=jax.ShapeDtypeStruct((total, 128), jnp.float32),
        compiler_params=pltpu.CompilerParams(vmem_limit_bytes=GRANT),
        name="window",
        cost_estimate=pl.CostEstimate(
            flops=2 * total * 640 * 512, bytes_accessed=4000000, transcendentals=total * 640
        ),
    )(who, q, four, two, one, paired, gates)


def far_scores(heads, device, core, q, kv_ref, s_ref, base, quarters):
    block = q.shape[0]
    zeros = jnp.zeros((block, 64), q.dtype)
    queries = (
        jnp.concatenate([q, zeros], axis=1),
        jnp.concatenate([q[:, :128], zeros, q[:, 128:]], axis=1),
    )
    token = base + lax.broadcasted_iota(jnp.int32, (block, 256), 0) // heads
    lane = lax.broadcasted_iota(jnp.int32, (1, 256), 1)
    top = None
    for quarter in range(quarters):
        for g in range(kv_ref.shape[0] // 8):
            some = slice(8 * g, 8 * g + 8)
            begin = 32 * quarter
            low = kv_ref[some, begin : begin + 32].reshape(256, 128)
            begin = 128 + 32 * (quarter % 2)
            high = kv_ref[some, begin : begin + 32].reshape(256, 128)
            s = nt(queries[quarter // 2], jnp.concatenate([low, high], axis=1))
            z = 4 * quarter + (lane % 32) // 8
            owner = (2 * z + core) * 16 + 8 * g + lane // 32
            end = (owner - device) * 128 + STRIDE * (lane % 8) + STRIDE - 1
            s = jnp.where(end <= token, s, LOW)
            slot = 2 * quarter + g
            s_ref[:, 256 * slot : 256 * slot + 256] = s
            most = jnp.maximum(s[:, :128], s[:, 128:])
            top = most if top is None else jnp.maximum(top, most)
    return jnp.maximum(jnp.max(top, axis=1, keepdims=True), FLOOR)


def far_mix(scale, s_ref, top, kv_ref, quarters):
    ones = jnp.ones((256, 128), jnp.bfloat16)
    accum = jnp.zeros((s_ref.shape[0], 256), jnp.float32)
    for quarter in range(quarters):
        for g in range(kv_ref.shape[0] // 8):
            slot = 2 * quarter + g
            s = s_ref[:, 256 * slot : 256 * slot + 256]
            p = jnp.exp2((s - top) * (scale * LOG2E)).astype(jnp.bfloat16)
            begin = 192 + 32 * quarter
            v = kv_ref[8 * g : 8 * g + 8, begin : begin + 32].reshape(256, 128)
            accum += jnp.dot(
                p, jnp.concatenate([v, ones], axis=1), preferred_element_type=jnp.float32
            )
    return accum


def skewed(scale, heads, who, core, q_ref, kv_ref, scratch, finish):
    sub = scratch[0].shape[0]
    blocks = q_ref.shape[0] // sub
    plane = who[2]

    def run(quarters):
        def score(j):
            return far_scores(
                heads,
                who[0],
                core,
                q_ref[j * sub : (j + 1) * sub],
                kv_ref,
                scratch[j % 2],
                j * (sub // heads),
                quarters,
            )

        tops = [score(0)]
        for j in range(blocks):
            if j + 1 < blocks:
                tops.append(score(j + 1))
            mix = far_mix(scale, scratch[j % 2], tops[j], kv_ref, quarters)
            finish(slice(j * sub, (j + 1) * sub), mix, tops[j])

    @pl.when(plane < 4)
    def _():
        run(1)

    @pl.when((plane >= 4) & (plane < 12))
    def _():
        run(3)

    @pl.when(plane >= 12)
    def _():
        run(4)


def first_kernel(scale, heads, who, q_ref, kv_ref, acc_ref, top_ref, *scratch):
    def finish(here, accum, top):
        acc_ref[here] = accum
        top_ref[here] = jnp.broadcast_to(top, (accum.shape[0], 128))

    skewed(scale, heads, who, who[1], q_ref, kv_ref, scratch, finish)


def second_kernel(
    scale,
    heads,
    who,
    q_ref,
    kv_ref,
    acc_ref,
    top_ref,
    win_ref,
    gate_ref,
    out_hbm,
    even,
    odd,
    result,
    sems,
):
    sub = even.shape[0]

    def move(j):
        here = slice(j * sub, (j + 1) * sub)
        return pltpu.make_async_copy(result.at[here], out_hbm.at[here], sems.at[j])

    def finish(here, accum, top):
        other = top_ref[here]
        most = jnp.maximum(other, top)
        grow = jnp.exp2((other - most) * (scale * LOG2E))
        shrink = jnp.exp2((top - most) * (scale * LOG2E))
        number = acc_ref[here, :128] * grow + accum[:, :128] * shrink
        total = acc_ref[here, 128:] * grow + accum[:, 128:] * shrink
        present = total > 0.0
        compressed = jnp.where(present, number / jnp.where(present, total, 1.0), 0.0)
        result[here] = (gate_ref[here, 0:1] * compressed + win_ref[here]).astype(result.dtype)
        move(here.start // sub).start()

    skewed(scale, heads, who, 1 - who[1], q_ref, kv_ref, (even, odd), finish)
    for j in range(q_ref.shape[0] // sub):
        move(j).wait()


def first_half(who, q, kv, scale, heads, sub=256):
    total = q.shape[0]
    keys = kv.shape[0] * 128
    inside = pl.BlockSpec(memory_space=pltpu.VMEM)
    return pl.pallas_call(
        functools.partial(first_kernel, scale, heads),
        in_specs=[pl.BlockSpec(memory_space=pltpu.SMEM), inside, inside],
        out_specs=[inside, inside],
        scratch_shapes=[pltpu.VMEM((sub, keys), jnp.float32)] * 2,
        out_shape=[
            jax.ShapeDtypeStruct((total, 256), jnp.float32),
            jax.ShapeDtypeStruct((total, 128), jnp.float32),
        ],
        compiler_params=pltpu.CompilerParams(vmem_limit_bytes=GRANT),
        name="first_half",
        cost_estimate=pl.CostEstimate(
            flops=2 * total * keys * 512, bytes_accessed=3000000, transcendentals=total * keys
        ),
    )(who, q, kv)


def second_half(who, q, kv, acc, top, win, gates, scale, heads, sub=256):
    total = q.shape[0]
    keys = kv.shape[0] * 128
    inside = pl.BlockSpec(memory_space=pltpu.VMEM)
    return pl.pallas_call(
        functools.partial(second_kernel, scale, heads),
        in_specs=[pl.BlockSpec(memory_space=pltpu.SMEM)] + [inside] * 6,
        out_specs=pl.BlockSpec(memory_space=pl.ANY),
        scratch_shapes=[
            pltpu.VMEM((sub, keys), jnp.float32),
            pltpu.VMEM((sub, keys), jnp.float32),
            pltpu.VMEM((total, 128), jnp.bfloat16),
            pltpu.SemaphoreType.DMA((total // sub,)),
        ],
        out_shape=jax.ShapeDtypeStruct((total, 128), jnp.bfloat16),
        compiler_params=pltpu.CompilerParams(vmem_limit_bytes=GRANT),
        name="second_half",
        cost_estimate=pl.CostEstimate(
            flops=2 * total * keys * 512, bytes_accessed=5000000, transcendentals=total * keys
        ),
    )(who, q, kv, acc, top, win, gates)


def local(
    queries, keys, values, key_first, key_second, value_first, value_second, gate_table, gate_index
):
    rows, heads, depth = queries.shape
    outer, inner = lax.axis_index("sa"), lax.axis_index("sb")
    core = outer % 2
    device = outer * lax.axis_size("sb") + inner
    who = jnp.stack([device, core, outer // 2]).astype(jnp.int32)
    planes = lax.axis_size("sa") // 2
    scale = depth ** (-0.5)

    def stay(x):
        return pltpu.with_memory_space_constraint(x, pltpu.HBM)

    paired = pair(stay(keys.T), stay(values))
    one = shifted(paired, ("sa", "sb"), 1)
    kfirst = key_first.T
    hidden, kfront, vfront = own_blocks(paired, kfirst, stay(value_first))
    payload = summary(
        one, hidden, kfront, stay(key_second), vfront, stay(value_second), planes
    )
    payload, later, again = lax.optimization_barrier((payload, one, paired))
    groups = [[2 * z + c for z in range(planes)] for c in range(2)]
    column = lax.all_to_all(payload, "sa", 0, 0, axis_index_groups=groups)
    four = shifted(again, ("sa", "sb"), 4)
    two = shifted(jnp.concatenate([later, again], axis=0), ("sa", "sb"), 2)
    query_rows = queries.reshape(rows * heads, depth)
    chosen = gate_index.reshape(rows * heads)
    onehot = (chosen[:, None] == lax.iota(jnp.int32, gate_table.shape[0])[None, :]).astype(
        jnp.float32
    )
    gates = jnp.sum(onehot[:, :, None] * gate_table[None, :, :], axis=1)
    copies = pack(column, lax.axis_size("sb"))
    mine = lax.all_to_all(copies, "sb", 0, 0)
    win = window_branch(who, query_rows, four, two, later, again, gates, scale, heads)
    mine, win = lax.optimization_barrier((mine, win))
    other = lax.ppermute(mine, "sa", [(i, i ^ 1) for i in range(2 * planes)])
    acc, top = first_half(who, query_rows, mine, scale, heads)
    mixed = second_half(who, query_rows, other, acc, top, win, gates, scale, heads)
    return mixed.reshape(rows, heads, values.shape[1])


def solution(mesh):
    in_specs = (
        P(("sa", "sb"), None, None),
        P(("sa", "sb"), None),
        P(("sa", "sb"), None),
        P(),
        P(),
        P(),
        P(),
        P(),
        P(("sa", "sb"), None),
    )
    out_specs = P(("sa", "sb"), None, None)
    return jax.shard_map(local, mesh=mesh, in_specs=in_specs, out_specs=out_specs, check_vma=False)
```

```python
import functools

import jax
import jax.numpy as jnp
from jax import lax
from jax.experimental import pallas as pl
from jax.experimental.pallas import tpu as pltpu
from jax.sharding import PartitionSpec as P


STRIDE = 16
LOG2E = 1.4426950408889634
LOW = -1e30
FLOOR = -1e29
GRANT = 20 << 20


def nt(a, b):
    return lax.dot_general(a, b, (((1,), (1,)), ((), ())), preferred_element_type=jnp.float32)


def shifted(shard, axis, by):
    size = lax.axis_size(axis)
    pairs = [(i, i + by) for i in range(size) if 0 <= i + by < size]
    return lax.ppermute(shard, axis, pairs)


def pair_kernel(keys_hbm, values_hbm, out_ref, keys, sems):
    loads = [
        pltpu.make_async_copy(keys_hbm, keys, sems.at[0]),
        pltpu.make_async_copy(values_hbm, out_ref.at[:, 256:], sems.at[1]),
    ]
    for load in loads:
        load.start()
    out_ref[:, 192:256] = jnp.zeros((out_ref.shape[0], 64), out_ref.dtype)
    loads[0].wait()
    out_ref[:, :192] = keys[...].astype(jnp.float32).T.astype(out_ref.dtype)
    loads[1].wait()


def pair(keys, values):
    keys = pltpu.with_memory_space_constraint(keys.T, pltpu.HBM)
    values = pltpu.with_memory_space_constraint(values, pltpu.HBM)
    return pl.pallas_call(
        pair_kernel,
        in_specs=[pl.BlockSpec(memory_space=pltpu.HBM)] * 2,
        out_specs=pl.BlockSpec(memory_space=pltpu.VMEM),
        out_shape=jax.ShapeDtypeStruct((values.shape[0], 384), keys.dtype),
        scratch_shapes=[pltpu.VMEM(keys.shape, keys.dtype), pltpu.SemaphoreType.DMA((2,))],
        compiler_params=pltpu.CompilerParams(vmem_limit_bytes=GRANT),
        name="pair",
    )(keys, values)


def silu(x):
    return x * (1.0 / (1.0 + jnp.exp(-x)))


def segments(wide_ref, count):
    keys, values = [], []
    for first in range(STRIDE):
        some = [wide_ref[part, pl.ds(first, count, stride=STRIDE), :] for part in range(3)]
        keys.append(jnp.concatenate([some[0], some[1][:, :64]], axis=1))
        values.append(some[2])
    keys = jnp.concatenate(keys, axis=1).astype(jnp.bfloat16)
    values = jnp.concatenate(values, axis=1).astype(jnp.bfloat16)
    return keys, values


def own_kernel(pair_ref, kfirst_ref, vfirst_ref, hidden_ref, wide):
    half_keys = kfirst_ref.shape[1] // 2
    half_values = vfirst_ref.shape[0] // 2
    count = pair_ref.shape[0] // STRIDE
    for part in range(3):
        lanes = slice(128 * part, 128 * part + 128)
        wide[part] = pair_ref[:, lanes].astype(jnp.float32)
    keys, values = segments(wide, count)
    nothing = jnp.zeros((count, 64), jnp.float32)
    back = jnp.concatenate(
        [
            nt(keys, kfirst_ref[:, half_keys:]),
            nothing,
            jnp.dot(values, vfirst_ref[half_values:], preferred_element_type=jnp.float32),
        ],
        axis=1,
    )
    ahead = jnp.concatenate(
        [
            nt(keys, kfirst_ref[:, :half_keys]),
            nothing,
            jnp.dot(values, vfirst_ref[:half_values], preferred_element_type=jnp.float32),
        ],
        axis=1,
    )
    row = lax.broadcasted_iota(jnp.int32, back.shape, 0)
    hidden_ref[...] = back + jnp.where(row == 0, 0.0, pltpu.roll(ahead, 1, 0))


def own_blocks(paired, kfirst, vfirst):
    rows = paired.shape[0]
    inside = pl.BlockSpec(memory_space=pltpu.VMEM)
    return pl.pallas_call(
        own_kernel,
        in_specs=[inside] * 3,
        out_specs=inside,
        out_shape=jax.ShapeDtypeStruct((rows // STRIDE, 384), jnp.float32),
        scratch_shapes=[pltpu.VMEM((3, rows, 128), jnp.float32)],
        compiler_params=pltpu.CompilerParams(vmem_limit_bytes=GRANT),
        name="own_blocks",
        cost_estimate=pl.CostEstimate(
            flops=1000000000, bytes_accessed=8000000, transcendentals=0
        ),
    )(paired, kfirst, vfirst)


def summary_kernel(
    before_ref, hidden_ref, kfirst_ref, ksecond_ref, vfirst_ref, vsecond_ref, out_ref, wide
):
    rows = before_ref.shape[0]
    count = hidden_ref.shape[0]
    for part in range(3):
        lanes = slice(128 * part, 128 * part + 128)
        wide[part] = before_ref[:, lanes].astype(jnp.float32)
    keys, values = segments(wide, rows // STRIDE)
    ahead = jnp.concatenate(
        [
            nt(keys, kfirst_ref[:, : kfirst_ref.shape[1] // 2]),
            jnp.zeros((count, 64), jnp.float32),
            jnp.dot(
                values,
                vfirst_ref[: vfirst_ref.shape[0] // 2],
                preferred_element_type=jnp.float32,
            ),
        ],
        axis=1,
    )
    row = lax.broadcasted_iota(jnp.int32, ahead.shape, 0)
    hidden = hidden_ref[...] + jnp.where(row == 0, pltpu.roll(ahead, 1, 0), 0.0)
    hidden = silu(hidden).astype(jnp.bfloat16)
    key = jnp.dot(hidden[:, :192], ksecond_ref[...], preferred_element_type=jnp.float32)
    value = jnp.dot(hidden[:, 256:], vsecond_ref[...], preferred_element_type=jnp.float32)
    high = jnp.concatenate([key[:, 128:], jnp.zeros((count, 64), jnp.float32)], axis=1)
    payload = jnp.concatenate([key[:, :128], high, value], axis=0).astype(out_ref.dtype)
    for copy in range(out_ref.shape[0]):
        out_ref[copy] = payload


def summary(before, hidden, kfirst, key_second, vfirst, value_second, copies):
    inside = pl.BlockSpec(memory_space=pltpu.VMEM)
    default = pl.BlockSpec()
    return pl.pallas_call(
        summary_kernel,
        in_specs=[inside, inside, inside, default, inside, default],
        out_specs=inside,
        out_shape=jax.ShapeDtypeStruct((copies, 3 * hidden.shape[0], 128), jnp.bfloat16),
        scratch_shapes=[pltpu.VMEM((3,) + (before.shape[0], 128), jnp.float32)],
        compiler_params=pltpu.CompilerParams(vmem_limit_bytes=GRANT),
        name="summary",
    )(before, hidden, kfirst, key_second, vfirst, value_second)


def pack_kernel(column_ref, out_hbm, packed, sems):
    planes = column_ref.shape[0]
    half = planes // 2
    count = column_ref.shape[1] // 3
    low = column_ref[:, :count].astype(jnp.float32).reshape(planes * count, 128)
    high = column_ref[:, count : 2 * count].astype(jnp.float32)
    high = jnp.concatenate(
        [
            high[:half].reshape(half * count, 128)[:, :64],
            high[half:].reshape(half * count, 128)[:, :64],
        ],
        axis=1,
    )
    value = column_ref[:, 2 * count :].astype(jnp.float32).reshape(planes * count, 128)
    packed[...] = jnp.concatenate([low, high, value], axis=0).astype(packed.dtype)
    moves = [
        pltpu.make_async_copy(packed, out_hbm.at[copy], sems.at[copy])
        for copy in range(out_hbm.shape[0])
    ]
    for move in moves:
        move.start()
    for move in moves:
        move.wait()


def pack(column, copies):
    planes, rows, lanes = column.shape
    size = planes * rows * 5 // 6
    return pl.pallas_call(
        pack_kernel,
        in_specs=[pl.BlockSpec(memory_space=pltpu.VMEM)],
        out_specs=pl.BlockSpec(memory_space=pl.ANY),
        out_shape=jax.ShapeDtypeStruct((copies, size, lanes), column.dtype),
        scratch_shapes=[
            pltpu.VMEM((size, lanes), column.dtype),
            pltpu.SemaphoreType.DMA((copies,)),
        ],
        compiler_params=pltpu.CompilerParams(vmem_limit_bytes=GRANT),
        name="pack",
    )(column)


def window_kernel(
    scale, heads, who, q_ref, four_ref, two_ref, one_ref, pair_ref, gate_ref, out_ref, *scratch
):
    sub = scratch[0].shape[0]
    size = pair_ref.shape[0]
    blocks = q_ref.shape[0] // sub
    device = who[0]
    base = pl.program_id(0) * (q_ref.shape[0] // heads)
    near = (
        jnp.concatenate([four_ref[...], two_ref[:size]], axis=0),
        jnp.concatenate([two_ref[size:], one_ref[...]], axis=0),
        pair_ref[...],
    )
    begins = [
        size * jnp.clip(4 - device, 0, 2),
        size * jnp.clip(2 - device, 0, 2),
    ]

    def score(j):
        s_ref = scratch[j % 2]
        q = q_ref[j * sub : (j + 1) * sub]
        q = jnp.concatenate([q, jnp.zeros((sub, 64), q.dtype)], axis=1)
        token = base + j * (sub // heads) + lax.broadcasted_iota(jnp.int32, (sub, 256), 0) // heads
        lane = lax.broadcasted_iota(jnp.int32, (sub, 256), 1)
        s0 = nt(q, near[0][:, :256])
        s0 = jnp.where(lane > jnp.maximum(token, begins[0] - 1), s0, LOW)
        s1 = nt(q, near[1][:, :256])
        s1 = jnp.where(lane >= begins[1], s1, LOW)
        s2 = nt(q, near[2][:, :256])
        s2 = jnp.where(lane[:, :128] <= token[:, :128], s2, LOW)
        s_ref[:, :256] = s0
        s_ref[:, 256:512] = s1
        s_ref[:, 512:] = s2
        top = jnp.maximum(jnp.maximum(s0, s1), jnp.concatenate([s2, s2], axis=1))
        return jnp.maximum(jnp.max(top, axis=1, keepdims=True), FLOOR)

    def mix(j, top):
        s_ref = scratch[j % 2]
        accum = jnp.zeros((sub, 256), jnp.float32)
        for part, at in enumerate((0, 256, 512)):
            wide = near[part].shape[0]
            p = jnp.exp2((s_ref[:, at : at + wide] - top) * (scale * LOG2E)).astype(jnp.bfloat16)
            v = jnp.concatenate([near[part][:, 256:], jnp.ones((wide, 128), jnp.bfloat16)], axis=1)
            accum += jnp.dot(p, v, preferred_element_type=jnp.float32)
        here = slice(j * sub, (j + 1) * sub)
        out_ref[here] = gate_ref[here, 1:2] * (accum[:, :128] / accum[:, 128:])

    tops = [score(0)]
    for j in range(blocks):
        if j + 1 < blocks:
            tops.append(score(j + 1))
        mix(j, tops[j])


def window_branch(who, q, four, two, one, paired, gates, scale, heads, block=1024, sub=256):
    total = q.shape[0]

    def row(width):
        return pl.BlockSpec((block, width), lambda i, w: (i, 0))

    def whole(array):
        return pl.BlockSpec(array.shape, lambda i, w: (0, 0))

    return pl.pallas_call(
        functools.partial(window_kernel, scale, heads),
        grid_spec=pltpu.PrefetchScalarGridSpec(
            num_scalar_prefetch=1,
            grid=(total // block,),
            in_specs=[
                row(q.shape[1]),
                whole(four),
                whole(two),
                whole(one),
                whole(paired),
                row(2),
            ],
            out_specs=row(128),
            scratch_shapes=[pltpu.VMEM((sub, 640), jnp.float32)] * 2,
        ),
        out_shape=jax.ShapeDtypeStruct((total, 128), jnp.float32),
        compiler_params=pltpu.CompilerParams(vmem_limit_bytes=GRANT),
        name="window",
        cost_estimate=pl.CostEstimate(
            flops=2 * total * 640 * 512, bytes_accessed=4000000, transcendentals=total * 640
        ),
    )(who, q, four, two, one, paired, gates)


def far_scores(heads, device, core, q, kv_ref, s_ref, base, quarters):
    block = q.shape[0]
    zeros = jnp.zeros((block, 64), q.dtype)
    queries = (
        jnp.concatenate([q, zeros], axis=1),
        jnp.concatenate([q[:, :128], zeros, q[:, 128:]], axis=1),
    )
    token = base + lax.broadcasted_iota(jnp.int32, (block, 256), 0) // heads
    lane = lax.broadcasted_iota(jnp.int32, (1, 256), 1)
    top = None
    for quarter in range(quarters):
        for g in range(kv_ref.shape[0] // 8):
            some = slice(8 * g, 8 * g + 8)
            begin = 32 * quarter
            low = kv_ref[some, begin : begin + 32].reshape(256, 128)
            begin = 128 + 32 * (quarter % 2)
            high = kv_ref[some, begin : begin + 32].reshape(256, 128)
            s = nt(queries[quarter // 2], jnp.concatenate([low, high], axis=1))
            z = 4 * quarter + (lane % 32) // 8
            owner = (2 * z + core) * 16 + 8 * g + lane // 32
            end = (owner - device) * 128 + STRIDE * (lane % 8) + STRIDE - 1
            s = jnp.where(end <= token, s, LOW)
            slot = 2 * quarter + g
            s_ref[:, 256 * slot : 256 * slot + 256] = s
            most = jnp.maximum(s[:, :128], s[:, 128:])
            top = most if top is None else jnp.maximum(top, most)
    return jnp.maximum(jnp.max(top, axis=1, keepdims=True), FLOOR)


def far_mix(scale, s_ref, top, kv_ref, quarters):
    ones = jnp.ones((256, 128), jnp.bfloat16)
    accum = jnp.zeros((s_ref.shape[0], 256), jnp.float32)
    for quarter in range(quarters):
        for g in range(kv_ref.shape[0] // 8):
            slot = 2 * quarter + g
            s = s_ref[:, 256 * slot : 256 * slot + 256]
            p = jnp.exp2((s - top) * (scale * LOG2E)).astype(jnp.bfloat16)
            begin = 192 + 32 * quarter
            v = kv_ref[8 * g : 8 * g + 8, begin : begin + 32].reshape(256, 128)
            accum += jnp.dot(
                p, jnp.concatenate([v, ones], axis=1), preferred_element_type=jnp.float32
            )
    return accum


def skewed(scale, heads, who, core, q_ref, kv_ref, scratch, finish):
    sub = scratch[0].shape[0]
    blocks = q_ref.shape[0] // sub
    plane = who[2]

    def run(quarters, first, count):
        def rows(j):
            return pl.ds(pl.multiple_of((first + j) * sub, sub), sub)

        def score(j):
            return far_scores(
                heads,
                who[0],
                core,
                q_ref[rows(j)],
                kv_ref,
                scratch[j % 2],
                (first + j) * (sub // heads),
                quarters,
            )

        tops = [score(0)]
        for j in range(count):
            if j + 1 < count:
                tops.append(score(j + 1))
            mix = far_mix(scale, scratch[j % 2], tops[j], kv_ref, quarters)
            finish(rows(j), first + j, mix, tops[j])

    def run_parts(quarters):
        half = blocks // 2

        @pl.loop(0, 2)
        def _(part):
            run(quarters, part * half, half)

    pl.when(plane < 4)(lambda: run(1, 0, blocks))
    pl.when((plane >= 4) & (plane < 8))(lambda: run_parts(2))
    pl.when((plane >= 8) & (plane < 12))(lambda: run_parts(3))
    pl.when(plane >= 12)(lambda: run(4, 0, blocks))


def first_kernel(scale, heads, who, q_ref, kv_ref, acc_ref, top_ref, *scratch):
    def finish(here, j, accum, top):
        acc_ref[here] = accum
        top_ref[here] = jnp.broadcast_to(top, (accum.shape[0], 128))

    skewed(scale, heads, who, who[1], q_ref, kv_ref, scratch, finish)


def second_kernel(
    scale,
    heads,
    who,
    q_ref,
    kv_ref,
    acc_ref,
    top_ref,
    win_ref,
    gate_ref,
    out_hbm,
    even,
    odd,
    result,
    sems,
):
    sub = even.shape[0]

    def move(j):
        here = pl.ds(pl.multiple_of(j * sub, sub), sub)
        return pltpu.make_async_copy(result.at[here], out_hbm.at[here], sems.at[j])

    def finish(here, j, accum, top):
        other = top_ref[here]
        most = jnp.maximum(other, top)
        grow = jnp.exp2((other - most) * (scale * LOG2E))
        shrink = jnp.exp2((top - most) * (scale * LOG2E))
        number = acc_ref[here, :128] * grow + accum[:, :128] * shrink
        total = acc_ref[here, 128:] * grow + accum[:, 128:] * shrink
        present = total > 0.0
        compressed = jnp.where(present, number / jnp.where(present, total, 1.0), 0.0)
        result[here] = (gate_ref[here, 0:1] * compressed + win_ref[here]).astype(result.dtype)
        move(j).start()

    skewed(scale, heads, who, 1 - who[1], q_ref, kv_ref, (even, odd), finish)
    for j in range(q_ref.shape[0] // sub):
        move(j).wait()


def first_half(who, q, kv, scale, heads, sub=256):
    total = q.shape[0]
    keys = kv.shape[0] * 128
    inside = pl.BlockSpec(memory_space=pltpu.VMEM)
    return pl.pallas_call(
        functools.partial(first_kernel, scale, heads),
        in_specs=[pl.BlockSpec(memory_space=pltpu.SMEM), inside, inside],
        out_specs=[inside, inside],
        scratch_shapes=[pltpu.VMEM((sub, keys), jnp.float32)] * 2,
        out_shape=[
            jax.ShapeDtypeStruct((total, 256), jnp.float32),
            jax.ShapeDtypeStruct((total, 128), jnp.float32),
        ],
        compiler_params=pltpu.CompilerParams(vmem_limit_bytes=GRANT),
        name="first_half",
        cost_estimate=pl.CostEstimate(
            flops=2 * total * keys * 512, bytes_accessed=3000000, transcendentals=total * keys
        ),
    )(who, q, kv)


def second_half(who, q, kv, acc, top, win, gates, scale, heads, sub=256):
    total = q.shape[0]
    keys = kv.shape[0] * 128
    inside = pl.BlockSpec(memory_space=pltpu.VMEM)
    return pl.pallas_call(
        functools.partial(second_kernel, scale, heads),
        in_specs=[pl.BlockSpec(memory_space=pltpu.SMEM)] + [inside] * 6,
        out_specs=pl.BlockSpec(memory_space=pl.ANY),
        scratch_shapes=[
            pltpu.VMEM((sub, keys), jnp.float32),
            pltpu.VMEM((sub, keys), jnp.float32),
            pltpu.VMEM((total, 128), jnp.bfloat16),
            pltpu.SemaphoreType.DMA((total // sub,)),
        ],
        out_shape=jax.ShapeDtypeStruct((total, 128), jnp.bfloat16),
        compiler_params=pltpu.CompilerParams(vmem_limit_bytes=GRANT),
        name="second_half",
        cost_estimate=pl.CostEstimate(
            flops=2 * total * keys * 512, bytes_accessed=5000000, transcendentals=total * keys
        ),
    )(who, q, kv, acc, top, win, gates)


def local(
    queries, keys, values, key_first, key_second, value_first, value_second, gate_table, gate_index
):
    rows, heads, depth = queries.shape
    outer, inner = lax.axis_index("sa"), lax.axis_index("sb")
    core = outer % 2
    device = outer * lax.axis_size("sb") + inner
    who = jnp.stack([device, core, outer // 2]).astype(jnp.int32)
    planes = lax.axis_size("sa") // 2
    scale = depth ** (-0.5)
    paired = pair(keys, values)
    one = shifted(paired, ("sa", "sb"), 1)
    kfirst = key_first.T
    hidden = own_blocks(paired, kfirst, value_first)
    payload = summary(one, hidden, kfirst, key_second, value_first, value_second, planes)
    payload, later, again = lax.optimization_barrier((payload, one, paired))
    groups = [[2 * z + c for z in range(planes)] for c in range(2)]
    column = lax.all_to_all(payload, "sa", 0, 0, axis_index_groups=groups)
    four = shifted(again, ("sa", "sb"), 4)
    two = shifted(jnp.concatenate([later, again], axis=0), ("sa", "sb"), 2)
    query_rows = queries.reshape(rows * heads, depth)
    chosen = gate_index.reshape(rows * heads)
    onehot = (chosen[:, None] == lax.iota(jnp.int32, gate_table.shape[0])[None, :]).astype(
        jnp.float32
    )
    gates = jnp.sum(onehot[:, :, None] * gate_table[None, :, :], axis=1)
    copies = pack(column, lax.axis_size("sb"))
    mine = lax.all_to_all(copies, "sb", 0, 0)
    win = window_branch(who, query_rows, four, two, later, again, gates, scale, heads)
    mine, win = lax.optimization_barrier((mine, win))
    other = lax.ppermute(mine, "sa", [(i, i ^ 1) for i in range(2 * planes)])
    acc, top = first_half(who, query_rows, mine, scale, heads)
    mixed = second_half(who, query_rows, other, acc, top, win, gates, scale, heads)
    return mixed.reshape(rows, heads, values.shape[1])


def solution(mesh):
    in_specs = (
        P(("sa", "sb"), None, None),
        P(("sa", "sb"), None),
        P(("sa", "sb"), None),
        P(),
        P(),
        P(),
        P(),
        P(),
        P(("sa", "sb"), None),
    )
    out_specs = P(("sa", "sb"), None, None)
    return jax.shard_map(local, mesh=mesh, in_specs=in_specs, out_specs=out_specs, check_vma=False)
```

```python
import functools

import jax
import jax.numpy as jnp
from jax import lax
from jax.experimental import pallas as pl
from jax.experimental.pallas import tpu as pltpu
from jax.sharding import PartitionSpec as P


STRIDE = 16
LOG2E = 1.4426950408889634
LOW = -1e30
FLOOR = -1e29
GRANT = 20 << 20


def nt(a, b):
    return lax.dot_general(a, b, (((1,), (1,)), ((), ())), preferred_element_type=jnp.float32)


def shifted(shard, axis, by):
    size = lax.axis_size(axis)
    pairs = [(i, i + by) for i in range(size) if 0 <= i + by < size]
    return lax.ppermute(shard, axis, pairs)


def pair_kernel(keys_hbm, values_hbm, out_ref, keys, sems):
    loads = [
        pltpu.make_async_copy(keys_hbm, keys, sems.at[0]),
        pltpu.make_async_copy(values_hbm, out_ref.at[:, 256:], sems.at[1]),
    ]
    for load in loads:
        load.start()
    out_ref[:, 192:256] = jnp.zeros((out_ref.shape[0], 64), out_ref.dtype)
    loads[0].wait()
    out_ref[:, :192] = keys[...].astype(jnp.float32).T.astype(out_ref.dtype)
    loads[1].wait()


def pair(keys, values):
    keys = pltpu.with_memory_space_constraint(keys.T, pltpu.HBM)
    values = pltpu.with_memory_space_constraint(values, pltpu.HBM)
    return pl.pallas_call(
        pair_kernel,
        in_specs=[pl.BlockSpec(memory_space=pltpu.HBM)] * 2,
        out_specs=pl.BlockSpec(memory_space=pltpu.VMEM),
        out_shape=jax.ShapeDtypeStruct((values.shape[0], 384), keys.dtype),
        scratch_shapes=[pltpu.VMEM(keys.shape, keys.dtype), pltpu.SemaphoreType.DMA((2,))],
        compiler_params=pltpu.CompilerParams(vmem_limit_bytes=GRANT),
        name="pair",
    )(keys, values)


def silu(x):
    return x * (1.0 / (1.0 + jnp.exp(-x)))


def segments(wide_ref, count):
    keys, values = [], []
    for first in range(STRIDE):
        some = [wide_ref[part, pl.ds(first, count, stride=STRIDE), :] for part in range(3)]
        keys.append(jnp.concatenate([some[0], some[1][:, :64]], axis=1))
        values.append(some[2])
    keys = jnp.concatenate(keys, axis=1).astype(jnp.bfloat16)
    values = jnp.concatenate(values, axis=1).astype(jnp.bfloat16)
    return keys, values


def own_kernel(pair_ref, kfirst_ref, vfirst_ref, hidden_ref, wide):
    half_keys = kfirst_ref.shape[1] // 2
    half_values = vfirst_ref.shape[0] // 2
    count = pair_ref.shape[0] // STRIDE
    for part in range(3):
        lanes = slice(128 * part, 128 * part + 128)
        wide[part] = pair_ref[:, lanes].astype(jnp.float32)
    keys, values = segments(wide, count)
    nothing = jnp.zeros((count, 64), jnp.float32)
    back = jnp.concatenate(
        [
            nt(keys, kfirst_ref[:, half_keys:]),
            nothing,
            jnp.dot(values, vfirst_ref[half_values:], preferred_element_type=jnp.float32),
        ],
        axis=1,
    )
    ahead = jnp.concatenate(
        [
            nt(keys, kfirst_ref[:, :half_keys]),
            nothing,
            jnp.dot(values, vfirst_ref[:half_values], preferred_element_type=jnp.float32),
        ],
        axis=1,
    )
    row = lax.broadcasted_iota(jnp.int32, back.shape, 0)
    hidden_ref[...] = back + jnp.where(row == 0, 0.0, pltpu.roll(ahead, 1, 0))


def own_blocks(paired, kfirst, vfirst):
    rows = paired.shape[0]
    inside = pl.BlockSpec(memory_space=pltpu.VMEM)
    return pl.pallas_call(
        own_kernel,
        in_specs=[inside] * 3,
        out_specs=inside,
        out_shape=jax.ShapeDtypeStruct((rows // STRIDE, 384), jnp.float32),
        scratch_shapes=[pltpu.VMEM((3, rows, 128), jnp.float32)],
        compiler_params=pltpu.CompilerParams(vmem_limit_bytes=GRANT),
        name="own_blocks",
        cost_estimate=pl.CostEstimate(
            flops=1000000000, bytes_accessed=8000000, transcendentals=0
        ),
    )(paired, kfirst, vfirst)


def summary_kernel(
    before_ref, hidden_ref, kfirst_ref, ksecond_ref, vfirst_ref, vsecond_ref, out_ref, wide
):
    rows = before_ref.shape[0]
    count = hidden_ref.shape[0]
    for part in range(3):
        lanes = slice(128 * part, 128 * part + 128)
        wide[part] = before_ref[:, lanes].astype(jnp.float32)
    keys, values = segments(wide, rows // STRIDE)
    ahead = jnp.concatenate(
        [
            nt(keys, kfirst_ref[:, : kfirst_ref.shape[1] // 2]),
            jnp.zeros((count, 64), jnp.float32),
            jnp.dot(
                values,
                vfirst_ref[: vfirst_ref.shape[0] // 2],
                preferred_element_type=jnp.float32,
            ),
        ],
        axis=1,
    )
    row = lax.broadcasted_iota(jnp.int32, ahead.shape, 0)
    hidden = hidden_ref[...] + jnp.where(row == 0, pltpu.roll(ahead, 1, 0), 0.0)
    hidden = silu(hidden).astype(jnp.bfloat16)
    key = jnp.dot(hidden[:, :192], ksecond_ref[...], preferred_element_type=jnp.float32)
    value = jnp.dot(hidden[:, 256:], vsecond_ref[...], preferred_element_type=jnp.float32)
    high = jnp.concatenate([key[:, 128:], jnp.zeros((count, 64), jnp.float32)], axis=1)
    payload = jnp.concatenate([key[:, :128], high, value], axis=0).astype(out_ref.dtype)
    for copy in range(out_ref.shape[0]):
        out_ref[copy] = payload


def summary(before, hidden, kfirst, key_second, vfirst, value_second, copies):
    inside = pl.BlockSpec(memory_space=pltpu.VMEM)
    default = pl.BlockSpec()
    return pl.pallas_call(
        summary_kernel,
        in_specs=[inside, inside, inside, default, inside, default],
        out_specs=inside,
        out_shape=jax.ShapeDtypeStruct((copies, 3 * hidden.shape[0], 128), jnp.bfloat16),
        scratch_shapes=[pltpu.VMEM((3,) + (before.shape[0], 128), jnp.float32)],
        compiler_params=pltpu.CompilerParams(vmem_limit_bytes=GRANT),
        name="summary",
    )(before, hidden, kfirst, key_second, vfirst, value_second)


def pack_kernel(column_ref, out_hbm, packed, sems):
    planes = column_ref.shape[0]
    half = planes // 2
    count = column_ref.shape[1] // 3
    low = column_ref[:, :count].astype(jnp.float32).reshape(planes * count, 128)
    high = column_ref[:, count : 2 * count].astype(jnp.float32)
    high = jnp.concatenate(
        [
            high[:half].reshape(half * count, 128)[:, :64],
            high[half:].reshape(half * count, 128)[:, :64],
        ],
        axis=1,
    )
    value = column_ref[:, 2 * count :].astype(jnp.float32).reshape(planes * count, 128)
    packed[...] = jnp.concatenate([low, high, value], axis=0).astype(packed.dtype)
    moves = [
        pltpu.make_async_copy(packed, out_hbm.at[copy], sems.at[copy])
        for copy in range(out_hbm.shape[0])
    ]
    for move in moves:
        move.start()
    for move in moves:
        move.wait()


def pack(column, copies):
    planes, rows, lanes = column.shape
    size = planes * rows * 5 // 6
    return pl.pallas_call(
        pack_kernel,
        in_specs=[pl.BlockSpec(memory_space=pltpu.VMEM)],
        out_specs=pl.BlockSpec(memory_space=pl.ANY),
        out_shape=jax.ShapeDtypeStruct((copies, size, lanes), column.dtype),
        scratch_shapes=[
            pltpu.VMEM((size, lanes), column.dtype),
            pltpu.SemaphoreType.DMA((copies,)),
        ],
        compiler_params=pltpu.CompilerParams(vmem_limit_bytes=GRANT),
        name="pack",
    )(column)


def window_kernel(
    scale, heads, who, q_ref, four_ref, two_ref, one_ref, pair_ref, gate_ref, out_ref, *scratch
):
    sub = scratch[0].shape[0]
    size = pair_ref.shape[0]
    blocks = q_ref.shape[0] // sub
    device = who[0]
    base = pl.program_id(0) * (q_ref.shape[0] // heads)
    near = (
        jnp.concatenate([four_ref[...], two_ref[:size]], axis=0),
        jnp.concatenate([two_ref[size:], one_ref[...]], axis=0),
        pair_ref[...],
    )
    begins = [
        size * jnp.clip(4 - device, 0, 2),
        size * jnp.clip(2 - device, 0, 2),
    ]

    def score(j):
        s_ref = scratch[j % 2]
        q = q_ref[j * sub : (j + 1) * sub]
        q = jnp.concatenate([q, jnp.zeros((sub, 64), q.dtype)], axis=1)
        token = base + j * (sub // heads) + lax.broadcasted_iota(jnp.int32, (sub, 256), 0) // heads
        lane = lax.broadcasted_iota(jnp.int32, (sub, 256), 1)
        s0 = nt(q, near[0][:, :256])
        s0 = jnp.where(lane > jnp.maximum(token, begins[0] - 1), s0, LOW)
        s1 = nt(q, near[1][:, :256])
        s1 = jnp.where(lane >= begins[1], s1, LOW)
        s2 = nt(q, near[2][:, :256])
        s2 = jnp.where(lane[:, :128] <= token[:, :128], s2, LOW)
        s_ref[:, :256] = s0
        s_ref[:, 256:512] = s1
        s_ref[:, 512:] = s2
        top = jnp.maximum(jnp.maximum(s0, s1), jnp.concatenate([s2, s2], axis=1))
        return jnp.maximum(jnp.max(top, axis=1, keepdims=True), FLOOR)

    def mix(j, top):
        s_ref = scratch[j % 2]
        accum = jnp.zeros((sub, 256), jnp.float32)
        for part, at in enumerate((0, 256, 512)):
            wide = near[part].shape[0]
            p = jnp.exp2((s_ref[:, at : at + wide] - top) * (scale * LOG2E)).astype(jnp.bfloat16)
            v = jnp.concatenate([near[part][:, 256:], jnp.ones((wide, 128), jnp.bfloat16)], axis=1)
            accum += jnp.dot(p, v, preferred_element_type=jnp.float32)
        here = slice(j * sub, (j + 1) * sub)
        out_ref[here] = gate_ref[here, 1:2] * (accum[:, :128] / accum[:, 128:])

    tops = [score(0)]
    for j in range(blocks):
        if j + 1 < blocks:
            tops.append(score(j + 1))
        mix(j, tops[j])


def window_branch(who, q, four, two, one, paired, gates, scale, heads, block=1024, sub=256):
    total = q.shape[0]

    def row(width):
        return pl.BlockSpec((block, width), lambda i, w: (i, 0))

    def whole(array):
        return pl.BlockSpec(array.shape, lambda i, w: (0, 0))

    return pl.pallas_call(
        functools.partial(window_kernel, scale, heads),
        grid_spec=pltpu.PrefetchScalarGridSpec(
            num_scalar_prefetch=1,
            grid=(total // block,),
            in_specs=[
                row(q.shape[1]),
                whole(four),
                whole(two),
                whole(one),
                whole(paired),
                row(2),
            ],
            out_specs=row(128),
            scratch_shapes=[pltpu.VMEM((sub, 640), jnp.float32)] * 2,
        ),
        out_shape=jax.ShapeDtypeStruct((total, 128), jnp.float32),
        compiler_params=pltpu.CompilerParams(vmem_limit_bytes=GRANT),
        name="window",
        cost_estimate=pl.CostEstimate(
            flops=2 * total * 640 * 512, bytes_accessed=4000000, transcendentals=total * 640
        ),
    )(who, q, four, two, one, paired, gates)


def far_scores(heads, device, core, q, kv_ref, s_ref, base, tiles):
    block = q.shape[0]
    zeros = jnp.zeros((block, 64), q.dtype)
    queries = (
        jnp.concatenate([q, zeros], axis=1),
        jnp.concatenate([q[:, :128], zeros, q[:, 128:]], axis=1),
    )
    token = base + lax.broadcasted_iota(jnp.int32, (block, 256), 0) // heads
    lane = lax.broadcasted_iota(jnp.int32, (1, 256), 1)
    top = None
    for tile in range(tiles):
        begin = 16 * tile
        low = kv_ref[:, begin : begin + 16].reshape(256, 128)
        begin = 128 + 16 * (tile % 4)
        high = kv_ref[:, begin : begin + 16].reshape(256, 128)
        s = nt(queries[tile // 4], jnp.concatenate([low, high], axis=1))
        z = 2 * tile + (lane % 16) // 8
        owner = (2 * z + core) * 16 + lane // 16
        end = (owner - device) * 128 + STRIDE * (lane % 8) + STRIDE - 1
        s = jnp.where(end <= token, s, LOW)
        s_ref[:, 256 * tile : 256 * tile + 256] = s
        most = jnp.maximum(s[:, :128], s[:, 128:])
        top = most if top is None else jnp.maximum(top, most)
    return jnp.maximum(jnp.max(top, axis=1, keepdims=True), FLOOR)


def far_mix(scale, s_ref, top, kv_ref, tiles):
    ones = jnp.ones((256, 128), jnp.bfloat16)
    accum = jnp.zeros((s_ref.shape[0], 256), jnp.float32)
    for tile in range(tiles):
        s = s_ref[:, 256 * tile : 256 * tile + 256]
        p = jnp.exp2((s - top) * (scale * LOG2E)).astype(jnp.bfloat16)
        begin = 192 + 16 * tile
        v = kv_ref[:, begin : begin + 16].reshape(256, 128)
        accum += jnp.dot(p, jnp.concatenate([v, ones], axis=1), preferred_element_type=jnp.float32)
    return accum


def skewed(scale, heads, who, core, q_ref, kv_ref, scratch, finish):
    sub = scratch[0].shape[0]
    blocks = q_ref.shape[0] // sub
    plane = who[2]

    def run(tiles, first, count):
        def rows(j):
            return pl.ds(pl.multiple_of((first + j) * sub, sub), sub)

        def score(j):
            return far_scores(
                heads,
                who[0],
                core,
                q_ref[rows(j)],
                kv_ref,
                scratch[j % 2],
                (first + j) * (sub // heads),
                tiles,
            )

        tops = [score(0)]
        for j in range(count):
            if j + 1 < count:
                tops.append(score(j + 1))
            mix = far_mix(scale, scratch[j % 2], tops[j], kv_ref, tiles)
            finish(rows(j), first + j, mix, tops[j])

    def run_parts(tiles):
        half = blocks // 2

        @pl.loop(0, 2)
        def _(part):
            run(tiles, part * half, half)

    begin = 0
    for until, tiles, whole in (
        (2, 1, True),
        (4, 2, False),
        (6, 3, True),
        (8, 4, False),
        (12, 6, False),
        (16, 8, True),
    ):
        here = (plane >= begin) & (plane < until)
        if whole:
            pl.when(here)(functools.partial(run, tiles, 0, blocks))
        else:
            pl.when(here)(functools.partial(run_parts, tiles))
        begin = until


def first_kernel(scale, heads, who, q_ref, kv_ref, acc_ref, top_ref, *scratch):
    def finish(here, j, accum, top):
        acc_ref[here] = accum
        top_ref[here] = jnp.broadcast_to(top, (accum.shape[0], 128))

    skewed(scale, heads, who, who[1], q_ref, kv_ref, scratch, finish)


def second_kernel(
    scale,
    heads,
    who,
    q_ref,
    kv_ref,
    acc_ref,
    top_ref,
    win_ref,
    gate_ref,
    out_hbm,
    even,
    odd,
    result,
    sems,
):
    sub = even.shape[0]

    def move(j):
        here = pl.ds(pl.multiple_of(j * sub, sub), sub)
        return pltpu.make_async_copy(result.at[here], out_hbm.at[here], sems.at[j])

    def finish(here, j, accum, top):
        other = top_ref[here]
        most = jnp.maximum(other, top)
        grow = jnp.exp2((other - most) * (scale * LOG2E))
        shrink = jnp.exp2((top - most) * (scale * LOG2E))
        number = acc_ref[here, :128] * grow + accum[:, :128] * shrink
        total = acc_ref[here, 128:] * grow + accum[:, 128:] * shrink
        present = total > 0.0
        compressed = jnp.where(present, number / jnp.where(present, total, 1.0), 0.0)
        result[here] = (gate_ref[here, 0:1] * compressed + win_ref[here]).astype(result.dtype)
        move(j).start()

    skewed(scale, heads, who, 1 - who[1], q_ref, kv_ref, (even, odd), finish)
    for j in range(q_ref.shape[0] // sub):
        move(j).wait()


def first_half(who, q, kv, scale, heads, sub=256):
    total = q.shape[0]
    keys = kv.shape[0] * 128
    inside = pl.BlockSpec(memory_space=pltpu.VMEM)
    return pl.pallas_call(
        functools.partial(first_kernel, scale, heads),
        in_specs=[pl.BlockSpec(memory_space=pltpu.SMEM), inside, inside],
        out_specs=[inside, inside],
        scratch_shapes=[pltpu.VMEM((sub, keys), jnp.float32)] * 2,
        out_shape=[
            jax.ShapeDtypeStruct((total, 256), jnp.float32),
            jax.ShapeDtypeStruct((total, 128), jnp.float32),
        ],
        compiler_params=pltpu.CompilerParams(vmem_limit_bytes=GRANT),
        name="first_half",
        cost_estimate=pl.CostEstimate(
            flops=2 * total * keys * 512, bytes_accessed=3000000, transcendentals=total * keys
        ),
    )(who, q, kv)


def second_half(who, q, kv, acc, top, win, gates, scale, heads, sub=256):
    total = q.shape[0]
    keys = kv.shape[0] * 128
    inside = pl.BlockSpec(memory_space=pltpu.VMEM)
    return pl.pallas_call(
        functools.partial(second_kernel, scale, heads),
        in_specs=[pl.BlockSpec(memory_space=pltpu.SMEM)] + [inside] * 6,
        out_specs=pl.BlockSpec(memory_space=pl.ANY),
        scratch_shapes=[
            pltpu.VMEM((sub, keys), jnp.float32),
            pltpu.VMEM((sub, keys), jnp.float32),
            pltpu.VMEM((total, 128), jnp.bfloat16),
            pltpu.SemaphoreType.DMA((total // sub,)),
        ],
        out_shape=jax.ShapeDtypeStruct((total, 128), jnp.bfloat16),
        compiler_params=pltpu.CompilerParams(vmem_limit_bytes=GRANT),
        name="second_half",
        cost_estimate=pl.CostEstimate(
            flops=2 * total * keys * 512, bytes_accessed=5000000, transcendentals=total * keys
        ),
    )(who, q, kv, acc, top, win, gates)


def local(
    queries, keys, values, key_first, key_second, value_first, value_second, gate_table, gate_index
):
    rows, heads, depth = queries.shape
    outer, inner = lax.axis_index("sa"), lax.axis_index("sb")
    core = outer % 2
    device = outer * lax.axis_size("sb") + inner
    who = jnp.stack([device, core, outer // 2]).astype(jnp.int32)
    planes = lax.axis_size("sa") // 2
    scale = depth ** (-0.5)
    paired = pair(keys, values)
    one = shifted(paired, ("sa", "sb"), 1)
    kfirst = key_first.T
    hidden = own_blocks(paired, kfirst, value_first)
    payload = summary(one, hidden, kfirst, key_second, value_first, value_second, planes)
    payload, later, again = lax.optimization_barrier((payload, one, paired))
    groups = [[2 * z + c for z in range(planes)] for c in range(2)]
    column = lax.all_to_all(payload, "sa", 0, 0, axis_index_groups=groups)
    four = shifted(again, ("sa", "sb"), 4)
    two = shifted(jnp.concatenate([later, again], axis=0), ("sa", "sb"), 2)
    query_rows = queries.reshape(rows * heads, depth)
    chosen = gate_index.reshape(rows * heads)
    onehot = (chosen[:, None] == lax.iota(jnp.int32, gate_table.shape[0])[None, :]).astype(
        jnp.float32
    )
    gates = jnp.sum(onehot[:, :, None] * gate_table[None, :, :], axis=1)
    copies = pack(column, lax.axis_size("sb"))
    mine = lax.all_to_all(copies, "sb", 0, 0)
    win = window_branch(who, query_rows, four, two, later, again, gates, scale, heads)
    mine, win = lax.optimization_barrier((mine, win))
    other = lax.ppermute(mine, "sa", [(i, i ^ 1) for i in range(2 * planes)])
    acc, top = first_half(who, query_rows, mine, scale, heads)
    mixed = second_half(who, query_rows, other, acc, top, win, gates, scale, heads)
    return mixed.reshape(rows, heads, values.shape[1])


def solution(mesh):
    in_specs = (
        P(("sa", "sb"), None, None),
        P(("sa", "sb"), None),
        P(("sa", "sb"), None),
        P(),
        P(),
        P(),
        P(),
        P(),
        P(("sa", "sb"), None),
    )
    out_specs = P(("sa", "sb"), None, None)
    return jax.shard_map(local, mesh=mesh, in_specs=in_specs, out_specs=out_specs, check_vma=False)
```
